32 devices in a mesh: group: 4 (over y, x), member: 8 (over z, core).
Axes of the slice: x: 2, y: 2, z: 4, core: 2. Of those that a mesh axis runs over, the one named last changes fastest.
Arguments:
- tokens: bfloat16 [4096, 1024], P(('group', 'member')), may hold values from -420 to 420
- latents: bfloat16 [1024, 1024], P('member'), may hold values from -420 to 420
- tok_gain: float32 [1024], replicated, may hold values from 0.5 to 1.5
- lat_gain: float32 [1024], replicated, may hold values from 0.5 to 1.5
- mlp_gain: float32 [1024], replicated, may hold values from 0.5 to 1.5
- w_ref_tok: bfloat16 [1024, 1024], replicated, may hold values from -1.15625 to 1.15625
- w_val_tok: bfloat16 [1024, 1024], replicated, may hold values from -0.75 to 0.75
- w_out_tok: bfloat16 [1024, 1024], replicated, may hold values from -0.1875 to 0.1875
- w_ref_lat: bfloat16 [1024, 1024], P('member'), may hold values from -1.15625 to 1.15625
- w_val_lat: bfloat16 [1024, 1024], P('member'), may hold values from -0.75 to 0.75
- w_out_lat: bfloat16 [1024, 1024], P('member'), may hold values from -0.1875 to 0.1875
- w_up: bfloat16 [1024, 2048], P(None, 'member'), may hold values from -0.1875 to 0.1875
- w_down: bfloat16 [2048, 1024], P('member'), may hold values from -0.125 to 0.125
Outputs:
- tokens_out: bfloat16 [4096, 1024], P(('group', 'member'))
- latents_out: bfloat16 [1024, 1024], P('member')
The draws below stay inside these ranges and needn't reach their ends.
All inputs are finite; a program needn't handle non-finite values.
Results may differ from the reference program's by a relative error of at most 0.005.
The reference program's roundings to bfloat16 on the way count: a program that leaves them out, or rounds other values in their place, can miss the bound.
Values may be sent and summed in bfloat16 or wider, within the bound.
No kernel may reach another device: no remote copies, remote signals or barrier semaphores. Data moves between devices by JAX's collectives and lax.ppermute only.
A program may use at most 128 MiB of HBM per device.

```python
import jax
import jax.numpy as jnp
from jax import lax

D = 1024
HEADS = 16
HEAD_DIM = 64
LATENTS = 1024
FF = 2048
TOKENS = 4096
N_GROUP = 4
N_MEMBER = 8


def latent_rows(key):
    base_rows = jnp.clip(jax.random.normal(jax.random.fold_in(key, 101), (LATENTS, D), jnp.float32), -4.0, 4.0)
    return base_rows


def draw_latents(key, part):
    lat_rows = latent_rows(key)
    return lat_rows.astype(jnp.bfloat16)


def draw_tokens(key, part):
    tok_rows = jnp.clip(jax.random.normal(jax.random.fold_in(key, 201), (TOKENS, D), jnp.float32), -4.0, 4.0)
    return tok_rows.astype(jnp.bfloat16)


def reference_pair(key):
    first_w = jnp.clip(jax.random.normal(jax.random.fold_in(key, 401), (D, D), jnp.float32), -5.0, 5.0) * D ** (-0.5)
    second_w = jnp.clip(jax.random.normal(jax.random.fold_in(key, 402), (D, D), jnp.float32), -5.0, 5.0) * D ** (-0.5)
    return (first_w * 1.6, second_w * 1.6)


def draw_w_ref_tok(key, part):
    return reference_pair(key)[0].astype(jnp.bfloat16)


def draw_w_ref_lat(key, part):
    return reference_pair(key)[1].astype(jnp.bfloat16)


def block_scale(stream_key, extent, split, smallest, largest):
    factor_of = 1.0
    for dim, blocks in split:
        draws = jax.random.uniform(jax.random.fold_in(jax.random.fold_in(stream_key, 6), dim), (blocks,), jnp.float32, smallest / len(split), largest / len(split))
        factor_of = factor_of * jnp.repeat(jnp.exp(draws), extent[dim] // blocks).reshape((-1,) + (1,) * (len(extent) - 1 - dim))
    return factor_of


def bell_draw(key, extent, width, reach, cuts=(), kind=jnp.bfloat16):
    gain = block_scale(key, extent, cuts, -0.22, 0.18) if cuts else 1.0
    drawn = jax.random.normal(key, extent, jnp.float32) * width * gain
    return jnp.minimum(jnp.maximum(drawn, -reach), reach).astype(kind)


def setup_inputs(seed: int = 0) -> dict:
    seeds = jax.random.split(jax.random.key(seed), 14)
    tokens = draw_tokens(jax.random.fold_in(seeds[13], 71), 0)
    latents = draw_latents(jax.random.fold_in(seeds[13], 71), 0)
    tok_gain = jnp.clip(1.0 + 0.1 * jax.random.normal(seeds[2], (D,), jnp.float32), 0.5, 1.5)
    lat_gain = jnp.clip(1.0 + 0.1 * jax.random.normal(seeds[3], (D,), jnp.float32), 0.5, 1.5)
    mlp_gain = jnp.clip(1.0 + 0.1 * jax.random.normal(seeds[4], (D,), jnp.float32), 0.5, 1.5)
    w_ref_tok = draw_w_ref_tok(jax.random.fold_in(seeds[13], 71), 0)
    w_val_tok = bell_draw(seeds[6], (D, D), (D // 16) ** -0.5, 0.75)
    w_out_tok = bell_draw(seeds[7], (D, D), D ** -0.5, 0.1875)
    w_ref_lat = draw_w_ref_lat(jax.random.fold_in(seeds[13], 71), 0)
    w_val_lat = bell_draw(seeds[9], (D, D), (D // 16) ** -0.5, 0.75, ((0, 8),))
    w_out_lat = bell_draw(seeds[10], (D, D), D ** -0.5, 0.1875, ((0, 8),))
    w_up = bell_draw(seeds[11], (D, FF), D ** -0.5, 0.1875, ((1, 8),))
    w_down = bell_draw(seeds[12], (FF, D), FF ** -0.5, 0.125, ((0, 8),))
    return dict(tokens=tokens, latents=latents, tok_gain=tok_gain, lat_gain=lat_gain, mlp_gain=mlp_gain, w_ref_tok=w_ref_tok, w_val_tok=w_val_tok, w_out_tok=w_out_tok, w_ref_lat=w_ref_lat, w_val_lat=w_val_lat, w_out_lat=w_out_lat, w_up=w_up, w_down=w_down)


NORM_EPS = 1e-06

def normalize(values):
    return values * lax.rsqrt(lax.optimization_barrier(jnp.mean(values * values, axis=-1, keepdims=True)) + NORM_EPS)

def project(left_side, right_side):
    return jnp.dot(left_side, right_side, preferred_element_type=jnp.float32)

def reference(tokens, latents, tok_gain, lat_gain, mlp_gain, w_ref_tok, w_val_tok, w_out_tok, w_ref_lat, w_val_lat, w_out_lat, w_up, w_down):
    score_scaling = HEAD_DIM ** (-0.5)
    lat_norm = (normalize(latents.astype(jnp.float32)) * lat_gain).astype(jnp.bfloat16)
    ref_lat = project(lat_norm, w_ref_lat).astype(jnp.bfloat16)
    val_lat = project(lat_norm, w_val_lat).astype(jnp.bfloat16)
    latent_key_rows = ref_lat.astype(jnp.float32).reshape(LATENTS, HEADS, HEAD_DIM)
    latent_value_rows = val_lat.astype(jnp.float32).reshape(LATENTS, HEADS, HEAD_DIM)
    block_count = N_GROUP * N_MEMBER
    row_count = TOKENS // block_count
    token_blocks = tokens.reshape(block_count, row_count, D)

    def advance(running, token_block):
        peak_now, total_now, summed_result = running
        tok_norm = (normalize(token_block.astype(jnp.float32)) * tok_gain).astype(jnp.bfloat16)
        ref_tok = project(tok_norm, w_ref_tok).astype(jnp.bfloat16)
        val_tok = project(tok_norm, w_val_tok).astype(jnp.bfloat16)
        query_rows = ref_tok.astype(jnp.float32).reshape(row_count, HEADS, HEAD_DIM)
        attention_scores = jnp.einsum('fxc,jxc->xfj', query_rows, latent_key_rows, precision=lax.Precision.HIGHEST) * score_scaling
        row_peak = lax.optimization_barrier(jnp.max(attention_scores, axis=2, keepdims=True))
        exponent = jnp.exp(attention_scores - row_peak)
        token_attention_weights = (exponent / lax.optimization_barrier(jnp.sum(exponent, axis=2, keepdims=True))).astype(jnp.bfloat16)
        token_attention = jnp.einsum('gei,igo->ego', token_attention_weights.astype(jnp.float32), latent_value_rows, precision=lax.Precision.HIGHEST)
        token_attention = token_attention.reshape(row_count, D).astype(jnp.bfloat16)
        tok_mid = token_block.astype(jnp.float32) + project(token_attention, w_out_tok)
        mlp_in = (normalize(tok_mid) * mlp_gain).astype(jnp.bfloat16)
        hidden = jax.nn.gelu(project(mlp_in, w_up), approximate=False).astype(jnp.bfloat16)
        tok_out = (tok_mid + project(hidden, w_down)).astype(jnp.bfloat16)
        peak_next = jnp.maximum(peak_now, lax.optimization_barrier(jnp.max(attention_scores, axis=1)))
        column_attention_weights = jnp.exp(attention_scores - peak_next[:, None, :])
        rescale_factor = jnp.exp(peak_now - peak_next)
        total_next = total_now * rescale_factor + lax.optimization_barrier(jnp.sum(column_attention_weights, axis=1))
        token_value_rows = val_tok.astype(jnp.float32).reshape(row_count, HEADS, HEAD_DIM)
        summed_result = summed_result * jnp.transpose(rescale_factor)[:, :, None] + jnp.einsum('gti,tgb->igb', column_attention_weights, token_value_rows, precision=lax.Precision.HIGHEST)
        return ((peak_next, total_next, summed_result), tok_out)
    start_state = (jnp.full((HEADS, LATENTS), -jnp.inf, dtype=jnp.float32), jnp.zeros((HEADS, LATENTS), jnp.float32), jnp.zeros((LATENTS, HEADS, HEAD_DIM), jnp.float32))
    final_state, tok_blocks = lax.scan(advance, start_state, token_blocks)
    col_total = final_state[1]
    col_sum = final_state[2]
    lat_attn = (col_sum / jnp.transpose(col_total)[:, :, None]).reshape(LATENTS, D)
    lat_mixed = normalize(lat_attn).astype(jnp.bfloat16)
    latents_out = (latents.astype(jnp.float32) + project(lat_mixed, w_out_lat)).astype(jnp.bfloat16)
    tokens_out = tok_blocks.reshape(TOKENS, D)
    return (tokens_out, latents_out)
```

```python
import functools

import jax
import jax.numpy as jnp
from jax import lax
from jax.experimental import pallas as pl
from jax.experimental.pallas import tpu as pltpu
from jax.sharding import PartitionSpec as P

HEAD_DIM = 64
NORM_EPS = 1e-06
SCORE_SCALE = HEAD_DIM ** (-0.5)
LOG2E = 1.4426950408889634
LN2 = 0.6931471805599453
STAT_LANES = 128
MLP_PEERS = 4


def normalize(values):
    return values * lax.rsqrt(jnp.mean(values * values, axis=-1, keepdims=True) + NORM_EPS)


def project(left_side, right_side):
    return jnp.dot(left_side, right_side, preferred_element_type=jnp.float32)


def project_t(left_side, right_side):
    return lax.dot_general(
        left_side, right_side, (((1,), (1,)), ((), ())), preferred_element_type=jnp.float32
    )


def swap(x, axis, offset):
    size = lax.axis_size(axis)
    return lax.ppermute(x, axis, [(i, i ^ offset) for i in range(size)])


def attention_kernel(heads, q_ref, v_ref, k_ref, u_ref, row_ref, col_ref, stat_ref):
    width = heads * HEAD_DIM
    rate = SCORE_SCALE * LOG2E
    q_all, v_all, k_all, u_all = q_ref[...], v_ref[...], k_ref[...], u_ref[...]
    n_tok, n_lat = q_all.shape[0], k_all.shape[0]
    lane = lax.broadcasted_iota(jnp.int32, (1, width), 1) // HEAD_DIM
    step = min(256, n_lat)
    row_step = min(256, n_tok)

    def only(values, head):
        return jnp.where(lane == head, values, jnp.zeros_like(values))

    stat_lane = lax.broadcasted_iota(jnp.int32, (1, STAT_LANES), 1)
    for first in range(0, n_lat, step):
        rows = slice(first, first + step)
        total_sum = jnp.zeros((step, width), jnp.float32)
        scale = jnp.zeros((step, width), jnp.float32)
        stats = jnp.zeros((step, STAT_LANES), jnp.float32)
        for head in range(heads):
            s = project_t(only(k_all[rows], head), q_all)
            peak = jnp.max(s, axis=1, keepdims=True)
            e = jnp.exp2((s - peak) * rate)
            total = jnp.sum(e, axis=1, keepdims=True)
            total_sum += project(e.astype(jnp.bfloat16), only(v_all, head))
            scale = jnp.where(lane == head, 1.0 / total, scale)
            stats = jnp.where(stat_lane == head, peak * rate + jnp.log2(total), stats)
        col_ref[rows, :] = total_sum * scale
        stat_ref[rows, :] = stats
    for first in range(0, n_tok, row_step):
        rows = slice(first, first + row_step)
        mixed = jnp.zeros((row_step, width), jnp.float32)
        for head in range(heads):
            s = project_t(only(q_all[rows], head), k_all)
            peak = jnp.max(s, axis=1, keepdims=True)
            e = jnp.exp2((s - peak) * rate)
            w = (e * (1.0 / jnp.sum(e, axis=1, keepdims=True))).astype(jnp.bfloat16)
            mixed += project(w, only(u_all, head))
        row_ref[rows, :] = mixed.astype(jnp.bfloat16)


def attention(q, v, k, u):
    n_tok, width = q.shape
    n_lat = k.shape[0]
    heads = width // HEAD_DIM
    return pl.pallas_call(
        functools.partial(attention_kernel, heads),
        out_shape=(
            jax.ShapeDtypeStruct((n_tok, width), jnp.bfloat16),
            jax.ShapeDtypeStruct((n_lat, width), jnp.float32),
            jax.ShapeDtypeStruct((n_lat, STAT_LANES), jnp.float32),
        ),
        in_specs=[pl.BlockSpec(memory_space=pltpu.VMEM)] * 4,
        out_specs=[pl.BlockSpec(memory_space=pltpu.VMEM)] * 3,
        cost_estimate=pl.CostEstimate(
            flops=10 * n_tok * n_lat * width,
            bytes_accessed=8 * (n_tok + n_lat) * width,
            transcendentals=2 * n_tok * n_lat * heads,
        ),
        name="attention",
    )(q, v, k, u)


def spread(stats, heads):
    rows = stats.shape[0]
    parts = [
        jnp.broadcast_to(stats[:, head : head + 1], (rows, HEAD_DIM)) for head in range(heads)
    ]
    return jnp.concatenate(parts, 1)


def merge(averages, stats):
    peak = functools.reduce(jnp.maximum, stats)
    weights = [jnp.exp2(s - peak) for s in stats]
    total = sum(weights)
    heads = averages[0].shape[1] // HEAD_DIM
    mixed = sum(
        a.astype(jnp.float32) * spread(w / total, heads) for a, w in zip(averages, weights)
    )
    return mixed, peak + jnp.log2(total)


def per_device(
    tokens,
    latents,
    tok_gain,
    lat_gain,
    mlp_gain,
    w_ref_tok,
    w_val_tok,
    w_out_tok,
    w_ref_lat,
    w_val_lat,
    w_out_lat,
    w_up,
    w_down,
):
    n_group, n_member = lax.axis_size("group"), lax.axis_size("member")
    n_z = n_member // 2
    g, m = lax.axis_index("group"), lax.axis_index("member")
    n_own, features = tokens.shape
    lat_own = latents.shape[0]
    width = features // n_group
    heads = width // HEAD_DIM
    share = lat_own // n_group
    ff_own = w_up.shape[1]
    ff_share = ff_own // n_group
    cols = g * width
    my_cols = functools.partial(lax.dynamic_slice_in_dim, start_index=cols, slice_size=width, axis=1)

    tok_near = [tokens] + [swap(tokens, "group", k) for k in range(1, n_group)]

    lat_norm = (normalize(latents.astype(jnp.float32)) * lat_gain).astype(jnp.bfloat16)
    lat_part = lax.dynamic_slice_in_dim(lat_norm, g * share, share, 0)
    lat_col = jnp.stack(
        [lat_part] + [swap(lat_part, "member", 2 * j) for j in range(1, n_z)]
    )
    w_mine = jnp.concatenate([my_cols(w_ref_lat), my_cols(w_val_lat), my_cols(w_out_lat)], 1)
    w_col = jnp.stack([w_mine] + [swap(w_mine, "member", 2 * j) for j in range(1, n_z)])
    lat_rows = jnp.stack([lat_col] + [swap(lat_col, "group", k) for k in range(1, n_group)])
    w_pair = jnp.stack([w_col, swap(w_col, "member", 1)], 1)
    order = jnp.arange(n_member) ^ m
    w_all = jnp.take(w_pair.reshape(n_member, lat_own, 3 * width), order, axis=0)
    w_all = w_all.reshape(features, 3 * width)

    ff_mine = jnp.stack(
        [
            jnp.transpose(lax.dynamic_slice_in_dim(w_up, g * ff_share, ff_share, 1)),
            lax.dynamic_slice_in_dim(w_down, g * ff_share, ff_share, 0),
        ]
    )
    ff_col = jnp.stack([ff_mine] + [swap(ff_mine, "member", 2 * j) for j in range(1, n_z)], 1)
    peers = min(n_group, MLP_PEERS)
    ff_plane = jnp.stack([ff_col] + [swap(ff_col, "group", k) for k in range(peers, n_group, peers)], 1)
    ff_all = jnp.stack([ff_plane, swap(ff_plane, "member", 1)], 1)
    up_t = ff_all[0].reshape(-1, features)
    down = ff_all[1].reshape(-1, features)

    tok_all = jnp.concatenate(tok_near, 0)
    tok_norm = (normalize(tok_all.astype(jnp.float32)) * tok_gain).astype(jnp.bfloat16)
    q = project(tok_norm, my_cols(w_ref_tok)).astype(jnp.bfloat16)
    v = project(tok_norm, my_cols(w_val_tok)).astype(jnp.bfloat16)

    kv_own = project(lat_rows.reshape(-1, features), w_all[:, : 2 * width]).astype(jnp.bfloat16)
    kv = jnp.concatenate([kv_own, swap(kv_own, "member", 1)], 0)

    row_out, col_avg, col_stat = attention(q, v, kv[:, :width], kv[:, width:])

    half = n_group * n_z * share
    far_avg, far_stat = swap(col_avg[half:], "member", 1), swap(col_stat[half:], "member", 1)
    pair_avg, pair_stat = merge([col_avg[:half], far_avg], [col_stat[:half], far_stat])
    pair_avg = pair_avg.astype(jnp.bfloat16).reshape(n_group, n_z, share, width)
    pair_stat = pair_stat.reshape(n_group, n_z, share, STAT_LANES)
    pieces = [(pair_avg[:, j].reshape(-1, width), pair_stat[:, j].reshape(-1, STAT_LANES)) for j in range(n_z)]
    for j in range(1, n_z):
        pieces[j] = (swap(pieces[j][0], "member", 2 * j), swap(pieces[j][1], "member", 2 * j))
    own_avg, _ = merge([a for a, _ in pieces], [s for _, s in pieces])
    group_order = jnp.arange(n_group) ^ g
    own_avg = jnp.take(own_avg.reshape(n_group, share, width), group_order, axis=0).reshape(lat_own, width)
    avg_near = jnp.stack([own_avg] + [swap(own_avg, "group", k) for k in range(1, n_group)])
    lat_attn = jnp.take(avg_near, group_order, axis=0)
    lat_attn = jnp.transpose(lat_attn, (1, 0, 2)).reshape(lat_own, features)
    lat_mixed = normalize(lat_attn).astype(jnp.bfloat16)
    lat_new = my_cols(latents).astype(jnp.float32) + project(lat_mixed, w_all[:, 2 * width :])
    lat_new = lat_new.astype(jnp.bfloat16)
    new_near = jnp.stack([lat_new] + [swap(lat_new, "group", k) for k in range(1, n_group)])
    latents_out = jnp.transpose(jnp.take(new_near, group_order, axis=0), (1, 0, 2))
    latents_out = latents_out.reshape(lat_own, features)

    row_blocks = row_out.reshape(n_group, n_own, width)
    swapped = [row_blocks[:peers]]
    for k in range(1, n_group):
        sent = jnp.stack([row_blocks[k ^ t] for t in range(peers)])
        swapped.append(swap(sent, "group", k))
    attn_mid = sum(
        project(
            part.reshape(-1, width),
            lax.dynamic_slice_in_dim(w_out_tok, (g ^ k) * width, width, 0),
        )
        for k, part in enumerate(swapped)
    )
    tok_mid = tok_all[: peers * n_own].astype(jnp.float32) + attn_mid
    mlp_in = (normalize(tok_mid) * mlp_gain).astype(jnp.bfloat16)
    hidden = jax.nn.gelu(project_t(mlp_in, up_t), approximate=False).astype(jnp.bfloat16)
    partial = project(hidden, down)
    result = tok_mid[:n_own] + partial[:n_own]
    for k in range(1, peers):
        sent = partial[k * n_own : (k + 1) * n_own].astype(jnp.bfloat16)
        result = result + swap(sent, "group", k).astype(jnp.float32)
    return (result.astype(jnp.bfloat16), latents_out)


def solution(mesh):
    in_specs = (
        P(("group", "member"), None),
        P("member", None),
        P(),
        P(),
        P(),
        P(),
        P(),
        P(),
        P("member", None),
        P("member", None),
        P("member", None),
        P(None, "member"),
        P("member", None),
    )
    out_specs = (P(("group", "member"), None), P("member", None))
    return jax.shard_map(
        per_device, mesh=mesh, in_specs=in_specs, out_specs=out_specs, check_vma=False
    )
```

```python
import functools

import jax
import jax.numpy as jnp
from jax import lax
from jax.experimental import pallas as pl
from jax.experimental.pallas import tpu as pltpu
from jax.sharding import PartitionSpec as P

HEAD_DIM = 64
NORM_EPS = 1e-06
LOG2E = 1.4426950408889634
RATE = HEAD_DIM ** (-0.5) * LOG2E
LANES = 128
MLP_PEERS = 4
BF16 = jnp.bfloat16
F32 = jnp.float32


VMEM = pl.BlockSpec(memory_space=pltpu.VMEM)
SMEM = pl.BlockSpec(memory_space=pltpu.SMEM)


def normalize(values):
    return values * lax.rsqrt(jnp.mean(values * values, axis=-1, keepdims=True) + NORM_EPS)


def project(left_side, right_side):
    return jnp.dot(left_side, right_side, preferred_element_type=F32)


def project_t(left_side, right_side):
    return lax.dot_general(
        left_side, right_side, (((1,), (1,)), ((), ())), preferred_element_type=F32
    )


def swap(x, axis, offset):
    size = lax.axis_size(axis)
    return lax.ppermute(x, axis, [(i, i ^ offset) for i in range(size)])


def gathered(x, axis, step, name):
    size = lax.axis_size(axis)
    with jax.named_scope(name):
        return [x] + [swap(x, axis, k) for k in range(step, size, step)]


def call(body, outs, ins, name, flops, scratch=(), nbytes=None):
    moved = sum(x.size * x.dtype.itemsize for x in ins) + sum(
        o.size * o.dtype.itemsize for o in outs
    )
    return pl.pallas_call(
        body,
        out_shape=outs,
        in_specs=[SMEM if x.dtype == jnp.int32 else VMEM for x in ins],
        out_specs=[VMEM] * len(outs),
        scratch_shapes=list(scratch),
        compiler_params=pltpu.CompilerParams(vmem_limit_bytes=48 * 1024 * 1024),
        cost_estimate=pl.CostEstimate(flops=flops, bytes_accessed=moved, transcendentals=0),
        name=name,
    )(*ins)


def aligned(index, multiple):
    return pl.multiple_of(index * multiple, multiple)


def shape(dims, dtype):
    return jax.ShapeDtypeStruct(dims, dtype)


def head_lanes(width):
    return lax.broadcasted_iota(jnp.int32, (1, width), 1) // HEAD_DIM


def only(values, lanes, head):
    return jnp.where(lanes == head, values, jnp.zeros_like(values))


def queries(tok_near, gain, w_ref, w_val, where, width):
    near = len(tok_near)
    n_own, features = tok_near[0].shape

    def body(*refs):
        pos, toks, gain_ref, ref_w, val_w = refs[0], refs[1 : 1 + near], *refs[1 + near : 4 + near]
        q_ref, v_ref, normed = refs[4 + near :]
        for k in range(near):
            rows = slice(k * n_own, (k + 1) * n_own)
            normed[rows, :] = (normalize(toks[k][...].astype(F32)) * gain_ref[...]).astype(BF16)
        q_ref[...] = project(normed[...], ref_w[...]).astype(BF16)
        v_ref[...] = project(normed[...], val_w[...]).astype(BF16)

    whole = [pl.BlockSpec((n_own, features), lambda i, pos: (0, 0))] * near
    gain_spec = pl.BlockSpec((1, features), lambda i, pos: (0, 0))
    col_spec = pl.BlockSpec((features, width), lambda i, pos: (0, pos[0]))
    out_spec = pl.BlockSpec((near * n_own, width), lambda i, pos: (0, 0))
    outs = (shape((near * n_own, width), BF16),) * 2
    if width % LANES == 0:
        return pl.pallas_call(
            body,
            out_shape=outs,
            grid_spec=pltpu.PrefetchScalarGridSpec(
                num_scalar_prefetch=1,
                grid=(1,),
                in_specs=[*whole, gain_spec, col_spec, col_spec],
                out_specs=[out_spec, out_spec],
                scratch_shapes=[pltpu.VMEM((near * n_own, features), BF16)],
            ),
            cost_estimate=pl.CostEstimate(
                flops=4 * near * n_own * features * width,
                bytes_accessed=2 * (near * n_own + 2 * width) * features,
                transcendentals=0,
            ),
            name="queries",
        )(where, *tok_near, gain.reshape(1, -1), w_ref, w_val)
    normed = (normalize(jnp.concatenate(tok_near, 0).astype(F32)) * gain).astype(BF16)
    cut = functools.partial(
        lax.dynamic_slice_in_dim, start_index=where[0] * width, slice_size=width, axis=1
    )
    return project(normed, cut(w_ref)).astype(BF16), project(normed, cut(w_val)).astype(BF16)


def weight_columns(w_ref, w_val, where, width):
    rows = w_ref.shape[0]
    if width % LANES == 0:

        def body(pos, a, b, out):
            out[:, :width] = a[...]
            out[:, width:] = b[...]

        spec = pl.BlockSpec((rows, width), lambda i, pos: (0, pos[0]))
        return pl.pallas_call(
            body,
            out_shape=shape((rows, 2 * width), BF16),
            grid_spec=pltpu.PrefetchScalarGridSpec(
                num_scalar_prefetch=1,
                grid=(1,),
                in_specs=[spec, spec],
                out_specs=pl.BlockSpec((rows, 2 * width), lambda i, pos: (0, 0)),
            ),
            name="weight_columns",
        )(where, w_ref, w_val)
    pad = ((0, 0), (0, LANES - width))
    return jnp.concatenate(
        [
            jnp.pad(lax.dynamic_slice_in_dim(w, where[0] * width, width, 1), pad)
            for w in (w_ref, w_val)
        ],
        1,
    )


def stack_rows(parts, name):
    rows, cols = parts[0].shape

    def body(*refs):
        for k, part in enumerate(refs[:-1]):
            refs[-1][k * rows : (k + 1) * rows, :] = part[...]

    return call(body, [shape((len(parts) * rows, cols), parts[0].dtype)], parts, name, 0)[0]


def keys(lat_near, w_own, w_far, where):
    near, n_z = len(lat_near), len(w_own)
    rows, features = lat_near[0].shape
    w_rows, cols = w_own[0].shape

    def body(*refs):
        pos, lats = refs[0], refs[1 : 1 + near]
        own, far = refs[1 + near : 1 + near + n_z], refs[1 + near + n_z : 1 + near + 2 * n_z]
        out, w_all, lat_all = refs[-3:]
        for core, pieces in enumerate((own, far)):
            for j, piece in enumerate(pieces):
                w_all[pl.ds(aligned(pos[1] ^ (2 * j + core), w_rows), w_rows), :] = piece[...]
        for k in range(near):
            lat_all[k * rows : (k + 1) * rows, :] = lats[k][...]
        out[...] = project(lat_all[...], w_all[...]).astype(BF16)

    return call(
        body,
        [shape((near * rows, cols), BF16)],
        [where, *lat_near, *w_own, *w_far],
        "keys",
        2 * near * rows * features * cols,
        [pltpu.VMEM((features, cols), BF16), pltpu.VMEM((near * rows, features), BF16)],
    )[0]


def columns(q, v, kv_own, kv_far):
    n_tok, width = q.shape
    half, pad2 = kv_own.shape
    pad = pad2 // 2
    heads = width // HEAD_DIM
    step = min(256, half)

    def body(q_ref, v_ref, own, far, own_out, far_out):
        q_all, v_all = q_ref[...], v_ref[...]
        lanes = head_lanes(width)
        stat_lanes = lax.broadcasted_iota(jnp.int32, (1, LANES), 1)
        for source, out in ((far, far_out), (own, own_out)):
            for first in range(0, half, step):
                rows = slice(first, first + step)
                k_rows = source[rows, :width]
                total_sum = jnp.zeros((step, width), F32)
                scale = jnp.zeros((step, width), F32)
                stats = jnp.zeros((step, LANES), F32)
                for head in range(heads):
                    s = project_t(only(k_rows, lanes, head), q_all)
                    peak = jnp.max(s, axis=1, keepdims=True)
                    e = jnp.exp2((s - peak) * RATE)
                    total = jnp.sum(e, axis=1, keepdims=True)
                    total_sum += project(e.astype(BF16), only(v_all, lanes, head))
                    scale = jnp.where(lanes == head, 1.0 / total, scale)
                    stats = jnp.where(stat_lanes == head, peak * RATE + jnp.log2(total), stats)
                out[rows, :width] = total_sum * scale
                if width < pad:
                    out[rows, width:pad] = jnp.zeros((step, pad - width), F32)
                out[rows, pad:] = stats

    outs = [shape((half, pad + LANES), F32)] * 2
    return call(body, outs, [q, v, kv_own, kv_far], "columns", 8 * half * n_tok * width * 2)


def rows_part(q, kv_own, kv_far, n_own, peers):
    n_tok, width = q.shape
    half, pad2 = kv_own.shape
    pad = pad2 // 2
    heads = width // HEAD_DIM
    near = n_tok // n_own

    def body(q_ref, own, far, *outs):
        lanes = head_lanes(width)
        for block in range(near):
            q_rows = q_ref[block * n_own : (block + 1) * n_own, :]
            mixed = jnp.zeros((n_own, width), F32)
            for head in range(heads):
                q_head = only(q_rows, lanes, head)
                s_own = project_t(q_head, own[:, :width])
                s_far = project_t(q_head, far[:, :width])
                peak = jnp.maximum(
                    jnp.max(s_own, axis=1, keepdims=True), jnp.max(s_far, axis=1, keepdims=True)
                )
                e_own = jnp.exp2((s_own - peak) * RATE)
                e_far = jnp.exp2((s_far - peak) * RATE)
                inverse = 1.0 / (
                    jnp.sum(e_own, axis=1, keepdims=True) + jnp.sum(e_far, axis=1, keepdims=True)
                )
                mixed += project(
                    (e_own * inverse).astype(BF16), only(own[:, pad : pad + width], lanes, head)
                )
                mixed += project(
                    (e_far * inverse).astype(BF16), only(far[:, pad : pad + width], lanes, head)
                )
            mixed = mixed.astype(BF16)
            for k in range(near):
                if block ^ k < peers:
                    t = block ^ k
                    outs[k][t * n_own : (t + 1) * n_own, :] = mixed

    outs = [shape((peers * n_own, width), BF16)] * near
    return call(body, outs, [q, kv_own, kv_far], "rows", 8 * half * n_tok * width * 2)


def spread(stats, heads):
    rows = stats.shape[0]
    return jnp.concatenate(
        [jnp.broadcast_to(stats[:, h : h + 1], (rows, HEAD_DIM)) for h in range(heads)], 1
    )


def weighted(parts, stats, heads):
    peak = functools.reduce(jnp.maximum, stats)
    weights = [jnp.exp2(s - peak) for s in stats]
    total = sum(weights)
    mixed = sum(a * spread(w / total, heads) for a, w in zip(parts, weights))
    return mixed, peak + jnp.log2(total)


def join_cores(own, far, near, n_z, share, width):
    pad = own.shape[1] - LANES
    heads = width // HEAD_DIM
    lat_own = near * share

    def body(own_ref, far_ref, *outs):
        for k in range(near):
            for j in range(n_z):
                rows = slice((k * n_z + j) * share, (k * n_z + j + 1) * share)
                to = slice(k * share, (k + 1) * share)
                mixed, stat = weighted(
                    [own_ref[rows, :width], far_ref[rows, :width]],
                    [own_ref[rows, pad:], far_ref[rows, pad:]],
                    heads,
                )
                high = stat.astype(BF16)
                rest = stat - high.astype(F32)
                middle = rest.astype(BF16)
                low = (rest - middle.astype(F32)).astype(BF16)
                outs[j][to, :width] = mixed.astype(BF16)
                if width < pad:
                    outs[j][to, width:pad] = jnp.zeros((share, pad - width), BF16)
                outs[j][to, pad : pad + LANES] = high
                outs[j][to, pad + LANES : pad + 2 * LANES] = middle
                outs[j][to, pad + 2 * LANES :] = low

    outs = [shape((lat_own, pad + 3 * LANES), BF16)] * n_z
    return call(body, outs, [own, far], "join_cores", 0)


def join_members(parts, where, near, share, width):
    lat_own = parts[0].shape[0]
    pad = parts[0].shape[1] - 3 * LANES
    heads = width // HEAD_DIM

    def body(*refs):
        pos, ins, out = refs[0], refs[1:-1], refs[-1]
        for k in range(near):
            rows = slice(k * share, (k + 1) * share)
            stats = [
                p[rows, pad : pad + LANES].astype(F32)
                + p[rows, pad + LANES : pad + 2 * LANES].astype(F32)
                + p[rows, pad + 2 * LANES :].astype(F32)
                for p in ins
            ]
            mixed, _ = weighted([p[rows, :width].astype(F32) for p in ins], stats, heads)
            out[pl.ds(aligned(pos[0] ^ k, share), share), :] = mixed

    return call(body, [shape((lat_own, width), F32)], [where, *parts], "join_members", 0)[0]


def latents_part(near_avg, lat_cols, own, far, where, n_share):
    near, n_z = len(near_avg), len(own)
    lat_own, width = near_avg[0].shape
    slab = own[0].shape[0] - 2 * n_share
    features = near * width

    def body(*refs):
        pos, avgs, lat = refs[0], refs[1 : 1 + near], refs[1 + near]
        own_w, far_w = refs[2 + near : 2 + near + n_z], refs[2 + near + n_z : 2 + near + 2 * n_z]
        out, w_all = refs[-2:]
        w_rows = near * slab
        for core, pieces in enumerate((own_w, far_w)):
            for j, piece in enumerate(pieces):
                for i in range(near):
                    to = aligned(pos[1] ^ (2 * j + core), w_rows) + i * slab
                    w_all[pl.ds(to, slab), :] = piece[
                        2 * n_share :, i * width : (i + 1) * width
                    ].astype(F32)
        values = [a[...] for a in avgs]
        square = sum(jnp.sum(a * a, axis=1, keepdims=True) for a in values)
        rate = lax.rsqrt(square * (1.0 / features) + NORM_EPS)
        total = lat[...].astype(F32)
        for k in range(near):
            total += project(
                (values[k] * rate).astype(BF16),
                w_all[pl.ds(aligned(pos[0] ^ k, width), width), :].astype(BF16),
            )
        out[...] = total.astype(BF16)

    return call(
        body,
        [shape((lat_own, width), BF16)],
        [where, *near_avg, lat_cols, *own, *far],
        "latents_part",
        2 * lat_own * features * width,
        [pltpu.VMEM((features, width), F32)],
    )[0]


def place_columns(parts, where):
    rows, width = parts[0].shape
    if width % LANES == 0:

        def body(*refs):
            for k, part in enumerate(refs[1:-1]):
                refs[-1][:, pl.ds(aligned(refs[0][0] ^ k, width), width)] = part[...]

        outs = [shape((rows, len(parts) * width), BF16)]
        return call(body, outs, [where, *parts], "place_columns", 0)[0]
    order = jnp.arange(len(parts)) ^ where[0]
    placed = jnp.take(jnp.stack(parts), order, axis=0)
    return jnp.transpose(placed, (1, 0, 2)).reshape(rows, -1)


def token_mlp(parts, tok_near, w_out, gain, own, far, where, n_share):
    near, peers, n_ff = len(parts), len(tok_near), len(own) + len(far)
    width = parts[0].shape[1]
    n_own, features = tok_near[0].shape

    def body(*refs):
        pos, w_ref, gain_ref = refs[:3]
        ins = refs[3 : 3 + near]
        toks = refs[3 + near : 3 + near + peers]
        ff = refs[3 + near + peers : 3 + near + peers + n_ff]
        own_out, sends = refs[3 + near + peers + n_ff], refs[4 + near + peers + n_ff : -2]
        up_t, down = refs[-2:]
        for i, piece in enumerate(ff):
            rows = slice(i * n_share, (i + 1) * n_share)
            up_t[rows, :] = piece[:n_share, :]
            down[rows, :] = piece[n_share : 2 * n_share, :]
        for t in range(peers):
            rows = slice(t * n_own, (t + 1) * n_own)
            mid = toks[t][...].astype(F32)
            for k in range(near):
                mid += project(
                    ins[k][rows, :], w_ref[pl.ds(aligned(pos[0] ^ k, width), width), :]
                )
            mlp_in = (normalize(mid) * gain_ref[...]).astype(BF16)
            hidden = project_t(mlp_in, up_t[...])
            hidden = (hidden * (0.5 + 0.5 * lax.erf(hidden * (0.5**0.5)))).astype(BF16)
            partial = project(hidden, down[...])
            if t == 0:
                own_out[...] = mid + partial
            else:
                sends[t - 1][...] = partial.astype(BF16)

    ff_rows = n_ff * n_share
    return call(
        body,
        [shape((n_own, features), F32)] + [shape((n_own, features), BF16)] * (peers - 1),
        [where, w_out, gain.reshape(1, -1), *parts, *tok_near, *own, *far],
        "token_mlp",
        2 * peers * n_own * features * (features + 2 * ff_rows),
        [pltpu.VMEM((ff_rows, features), BF16)] * 2,
    )


def add_up(own, received):
    def body(*refs):
        refs[-1][...] = sum(r[...].astype(F32) for r in refs[:-1]).astype(BF16)

    return call(body, [shape(own.shape, BF16)], [own, *received], "add_up", 0)[0]


def per_device(
    tokens,
    latents,
    tok_gain,
    lat_gain,
    mlp_gain,
    w_ref_tok,
    w_val_tok,
    w_out_tok,
    w_ref_lat,
    w_val_lat,
    w_out_lat,
    w_up,
    w_down,
):
    n_group, n_member = lax.axis_size("group"), lax.axis_size("member")
    n_z = n_member // 2
    g, m = lax.axis_index("group"), lax.axis_index("member")
    where = jnp.stack([g, m]).astype(jnp.int32)
    n_own, features = tokens.shape
    lat_own = latents.shape[0]
    width = features // n_group
    share = lat_own // n_group
    ff_share = w_up.shape[1] // n_group
    peers = min(n_group, MLP_PEERS)
    cut = lax.dynamic_slice_in_dim

    tok_near = gathered(tokens, "group", 1, "tok")
    lat_part = (normalize(cut(latents, g * share, share, 0).astype(F32)) * lat_gain).astype(BF16)
    lat_col = gathered(lat_part, "member", 2, "latz")
    w_own = gathered(weight_columns(w_ref_lat, w_val_lat, where, width), "member", 2, "wz")
    w_far = [swap(w, "member", 1) for w in w_own]
    lat_near = gathered(stack_rows(lat_col, "stack_lat"), "group", 1, "latg")

    w_slab = cut(w_out_lat, g * width, width, 1)
    slab = w_slab.shape[0] // n_group
    ff_mine = jnp.concatenate(
        [
            jnp.transpose(cut(w_up, g * ff_share, ff_share, 1)),
            cut(w_down, g * ff_share, ff_share, 0),
            jnp.concatenate([w_slab[i * slab : (i + 1) * slab] for i in range(n_group)], 1),
        ],
        0,
    )
    ff_own = gathered(ff_mine, "member", 2, "ffz")
    ff_far = [swap(f, "member", 1) for f in ff_own]
    extra = [swap(f, "group", k) for k in range(peers, n_group, peers) for f in ff_own]
    extra_far = [swap(f, "member", 1) for f in extra]

    q, v = queries(tok_near, tok_gain, w_ref_tok, w_val_tok, where, width)
    kv_own = keys(lat_near, w_own, w_far, where)
    kv_far = swap(kv_own, "member", 1)

    col_own, col_far = columns(q, v, kv_own, kv_far)
    col_got = swap(col_far, "member", 1)
    row_parts = rows_part(q, kv_own, kv_far, n_own, peers)
    pieces = join_cores(col_own, col_got, n_group, n_z, share, width)
    with jax.named_scope("colz"):
        pieces = [pieces[0]] + [swap(pieces[j], "member", 2 * j) for j in range(1, n_z)]
    with jax.named_scope("rowg"):
        row_parts = [row_parts[0]] + [swap(row_parts[k], "group", k) for k in range(1, n_group)]
    own_avg = join_members(pieces, where, n_group, share, width)
    avg_near = gathered(own_avg, "group", 1, "avgg")
    mid, *sends = token_mlp(
        row_parts,
        tok_near[:peers],
        w_out_tok,
        mlp_gain,
        ff_own + extra,
        ff_far + extra_far,
        where,
        ff_share,
    )
    with jax.named_scope("mlpg"):
        received = [swap(s, "group", k + 1) for k, s in enumerate(sends)]
    lat_cols = cut(latents, g * width, width, 1)
    lat_new = latents_part(avg_near, lat_cols, ff_own, ff_far, where, ff_share)
    latents_out = place_columns(gathered(lat_new, "group", 1, "latout"), where)
    tokens_out = add_up(mid, received)
    return (tokens_out, latents_out)


def solution(mesh):
    in_specs = (
        P(("group", "member"), None),
        P("member", None),
        P(),
        P(),
        P(),
        P(),
        P(),
        P(),
        P("member", None),
        P("member", None),
        P("member", None),
        P(None, "member"),
        P("member", None),
    )
    out_specs = (P(("group", "member"), None), P("member", None))
    return jax.shard_map(
        per_device, mesh=mesh, in_specs=in_specs, out_specs=out_specs, check_vma=False
    )
```

```python
import functools

import jax
import jax.numpy as jnp
from jax import lax
from jax.experimental import pallas as pl
from jax.experimental.pallas import tpu as pltpu
from jax.sharding import PartitionSpec as P


HEAD_DIM = 64
NORM_EPS = 1e-06
LOG2E = 1.4426950408889634
RATE = HEAD_DIM ** (-0.5) * LOG2E
LANES = 128
MLP_PEERS = 4
BF16 = jnp.bfloat16
F32 = jnp.float32


VMEM = pl.BlockSpec(memory_space=pltpu.VMEM)
SMEM = pl.BlockSpec(memory_space=pltpu.SMEM)


def normalize(values):
    return values * lax.rsqrt(jnp.mean(values * values, axis=-1, keepdims=True) + NORM_EPS)


def project(left_side, right_side):
    return jnp.dot(left_side, right_side, preferred_element_type=F32)


def project_t(left_side, right_side):
    return lax.dot_general(
        left_side, right_side, (((1,), (1,)), ((), ())), preferred_element_type=F32
    )


def swap(x, axis, offset):
    size = lax.axis_size(axis)
    return lax.ppermute(x, axis, [(i, i ^ offset) for i in range(size)])


def gathered(x, axis, step):
    size = lax.axis_size(axis)
    return [x] + [swap(x, axis, k) for k in range(step, size, step)]


def call(body, outs, ins, flops, scratch=()):
    moved = sum(x.size * x.dtype.itemsize for x in ins) + sum(
        o.size * o.dtype.itemsize for o in outs
    )
    return pl.pallas_call(
        body,
        out_shape=outs,
        in_specs=[SMEM if x.dtype == jnp.int32 else VMEM for x in ins],
        out_specs=[VMEM] * len(outs),
        scratch_shapes=list(scratch),
        compiler_params=pltpu.CompilerParams(vmem_limit_bytes=48 * 1024 * 1024),
        cost_estimate=pl.CostEstimate(flops=flops, bytes_accessed=moved, transcendentals=0),
    )(*ins)


def aligned(index, multiple):
    return pl.multiple_of(index * multiple, multiple)


def shape(dims, dtype):
    return jax.ShapeDtypeStruct(dims, dtype)


def head_lanes(width):
    return lax.broadcasted_iota(jnp.int32, (1, width), 1) // HEAD_DIM


def only(values, lanes, head):
    return jnp.where(lanes == head, values, jnp.zeros_like(values))


def side_by_side(pair, width):
    pad = ((0, 0), (0, -width % LANES))
    return jnp.concatenate([jnp.pad(w, pad) for w in pair], 1)


def from_group(x, where, size, dim):
    return lax.dynamic_slice_in_dim(x, where[0] * size, size, dim)


def queries(tok_near, gain, w_ref, w_val, where, width):
    near = len(tok_near)
    n_own, features = tok_near[0].shape
    if width % LANES:
        normed = (normalize(jnp.concatenate(tok_near, 0).astype(F32)) * gain).astype(BF16)
        return side_by_side(
            [project(normed, from_group(w, where, width, 1)).astype(BF16) for w in (w_ref, w_val)],
            width,
        )

    def body(*refs):
        toks, gain_ref, ref_w, val_w = refs[1 : 1 + near], *refs[1 + near : 4 + near]
        out, normed = refs[4 + near :]
        for k in range(near):
            rows = slice(k * n_own, (k + 1) * n_own)
            normed[rows, :] = (normalize(toks[k][...].astype(F32)) * gain_ref[...]).astype(BF16)
        out[:, :width] = project(normed[...], ref_w[...]).astype(BF16)
        out[:, width:] = project(normed[...], val_w[...]).astype(BF16)

    col_spec = pl.BlockSpec((features, width), lambda i, pos: (0, pos[0]))
    return pl.pallas_call(
        body,
        out_shape=shape((near * n_own, 2 * width), BF16),
        grid_spec=pltpu.PrefetchScalarGridSpec(
            num_scalar_prefetch=1,
            grid=(1,),
            in_specs=[
                *[pl.BlockSpec((n_own, features), lambda i, pos: (0, 0))] * near,
                pl.BlockSpec((1, features), lambda i, pos: (0, 0)),
                col_spec,
                col_spec,
            ],
            out_specs=pl.BlockSpec((near * n_own, 2 * width), lambda i, pos: (0, 0)),
            scratch_shapes=[pltpu.VMEM((near * n_own, features), BF16)],
        ),
        cost_estimate=pl.CostEstimate(
            flops=4 * near * n_own * features * width,
            bytes_accessed=2 * (near * n_own + 2 * width) * features,
            transcendentals=0,
        ),
        name="queries",
    )(where, *tok_near, gain.reshape(1, -1), w_ref, w_val)


def prepare(latents, gain, w_ref, w_val, w_out, w_up, w_down, where):
    n_group = lax.axis_size("group")
    rows, features = latents.shape
    share, width = rows // n_group, features // n_group
    ff = w_up.shape[1] // n_group
    w_rows = w_ref.shape[0]
    slab = w_rows // n_group
    if width % LANES or share % 16 or slab % 16 or ff % 16 or LANES % ff:
        lat = normalize(from_group(latents, where, share, 0).astype(F32)) * gain
        out_cols = from_group(w_out, where, width, 1)
        return (
            lat.astype(BF16),
            side_by_side([from_group(w, where, width, 1) for w in (w_ref, w_val)], width),
            jnp.concatenate(
                [
                    jnp.transpose(from_group(w_up, where, ff, 1)),
                    from_group(w_down, where, ff, 0),
                    jnp.concatenate(
                        [out_cols[i * slab : (i + 1) * slab] for i in range(n_group)], 1
                    ),
                ],
                0,
            ),
        )

    def body(pos, lat_ref, gain_ref, ref_w, val_w, out_w, up_w, down_w, lat, cols, rest, turned):
        lat[...] = (normalize(lat_ref[...].astype(F32)) * gain_ref[...]).astype(BF16)
        cols[:, :width] = ref_w[...]
        cols[:, width:] = val_w[...]
        turned[...] = jnp.transpose(up_w[...].astype(F32))
        first = aligned(lax.rem(pos[0], LANES // ff), ff)
        rest[:ff, :] = turned[pl.ds(first, ff), :].astype(BF16)
        rest[ff : 2 * ff, :] = down_w[...]
        for i in range(n_group):
            rest[2 * ff :, i * width : (i + 1) * width] = out_w[i * slab : (i + 1) * slab, :]

    col_spec = pl.BlockSpec((w_rows, width), lambda i, pos: (0, pos[0]))
    outs = ((share, features), (w_rows, 2 * width), (2 * ff + slab, features))
    return pl.pallas_call(
        body,
        out_shape=[shape(o, BF16) for o in outs],
        grid_spec=pltpu.PrefetchScalarGridSpec(
            num_scalar_prefetch=1,
            grid=(1,),
            in_specs=[
                pl.BlockSpec((share, features), lambda i, pos: (pos[0], 0)),
                pl.BlockSpec((1, features), lambda i, pos: (0, 0)),
                col_spec,
                col_spec,
                col_spec,
                pl.BlockSpec((features, LANES), lambda i, pos: (0, pos[0] // (LANES // ff))),
                pl.BlockSpec((ff, features), lambda i, pos: (pos[0], 0)),
            ],
            out_specs=[pl.BlockSpec(o, lambda i, pos: (0, 0)) for o in outs],
            scratch_shapes=[pltpu.VMEM((LANES, features), F32)],
        ),
        cost_estimate=pl.CostEstimate(flops=0, bytes_accessed=4 * 1024 * 1024, transcendentals=0),
        name="prepare",
    )(where, latents, gain.reshape(1, -1), w_ref, w_val, w_out, w_up, w_down)


def stack_rows(parts):
    rows, cols = parts[0].shape

    def body(*refs):
        for k, part in enumerate(refs[:-1]):
            refs[-1][k * rows : (k + 1) * rows, :] = part[...]

    return call(body, [shape((len(parts) * rows, cols), parts[0].dtype)], parts, 0)[0]


def keys(lat_near, w_own, w_far, where):
    near, n_z = len(lat_near), len(w_own)
    rows, features = lat_near[0].shape
    w_rows, cols = w_own[0].shape

    def body(*refs):
        pos, lats = refs[0], refs[1 : 1 + near]
        own, far = refs[1 + near : 1 + near + n_z], refs[1 + near + n_z : 1 + near + 2 * n_z]
        out, w_all, lat_all = refs[-3:]
        for core, pieces in enumerate((own, far)):
            for j, piece in enumerate(pieces):
                w_all[pl.ds(aligned(pos[1] ^ (2 * j + core), w_rows), w_rows), :] = piece[...]
        for k in range(near):
            lat_all[k * rows : (k + 1) * rows, :] = lats[k][...]
        out[...] = project(lat_all[...], w_all[...]).astype(BF16)

    return call(
        body,
        [shape((near * rows, cols), BF16)],
        [where, *lat_near, *w_own, *w_far],
        2 * near * rows * features * cols,
        [pltpu.VMEM((features, cols), BF16), pltpu.VMEM((near * rows, features), BF16)],
    )[0]


def columns(qv_own, qv_far, kv_own, near, n_z, share, width):
    n_tok, pad = qv_own.shape[0], qv_own.shape[1] // 2
    heads = width // HEAD_DIM
    block = n_z * share
    group = 2 if near % 2 == 0 else 1
    step = group * block

    def body(own, far, k_ref, *outs):
        lanes = head_lanes(width)
        stat_lanes = lax.broadcasted_iota(jnp.int32, (1, LANES), 1)
        for first in range(0, near, group):
            k_rows = k_ref[first * block : first * block + step, :width]
            mixed = jnp.zeros((step, width), F32)
            scale = jnp.zeros((step, width), F32)
            stats = jnp.zeros((step, LANES), F32)
            for head in range(heads):
                k_head = only(k_rows, lanes, head)
                scores = [project_t(k_head, qv[:, :width]) for qv in (own, far)]
                peak = jnp.maximum(*[jnp.max(s, axis=1, keepdims=True) for s in scores])
                powers = [jnp.exp2((s - peak) * RATE) for s in scores]
                total = sum(jnp.sum(e, axis=1, keepdims=True) for e in powers)
                for e, qv in zip(powers, (own, far)):
                    mixed += project(e.astype(BF16), only(qv[:, pad : pad + width], lanes, head))
                scale = jnp.where(lanes == head, 1.0 / total, scale)
                stats = jnp.where(stat_lanes == head, peak * RATE + jnp.log2(total), stats)
            mixed = (mixed * scale).astype(BF16)
            high = stats.astype(BF16).astype(F32)
            middle = (stats - high).astype(BF16).astype(F32)
            low = stats - high - middle
            packed = high + pltpu.roll(middle, 32, 1) + pltpu.roll(low, 64, 1)
            packed = packed.astype(BF16)
            for k in range(group):
                for j in range(n_z):
                    rows = slice(k * block + j * share, k * block + (j + 1) * share)
                    to = slice((first + k) * share, (first + k + 1) * share)
                    outs[j][to, :width] = mixed[rows]
                    if width < pad:
                        outs[j][to, width:pad] = jnp.zeros((share, pad - width), BF16)
                    outs[j][to, pad:] = packed[rows]

    outs = [shape((near * share, pad + LANES), BF16)] * n_z
    flops = 16 * near * block * n_tok * width
    return call(body, outs, [qv_own, qv_far, kv_own], flops)


def rows_part(qv, kv_own, kv_far, width, n_own, peers):
    n_tok = qv.shape[0]
    half, pad2 = kv_own.shape
    pad = pad2 // 2
    heads = width // HEAD_DIM
    near = n_tok // n_own

    def body(q_ref, own, far, *outs):
        lanes = head_lanes(width)
        group = 2 if near % 2 == 0 else 1
        for first in range(0, near, group):
            q_rows = q_ref[first * n_own : (first + group) * n_own, :width]
            mixed = jnp.zeros((group * n_own, width), F32)
            for head in range(heads):
                q_head = only(q_rows, lanes, head)
                s_own = project_t(q_head, own[:, :width])
                s_far = project_t(q_head, far[:, :width])
                peak = jnp.maximum(
                    jnp.max(s_own, axis=1, keepdims=True), jnp.max(s_far, axis=1, keepdims=True)
                )
                e_own = jnp.exp2((s_own - peak) * RATE)
                e_far = jnp.exp2((s_far - peak) * RATE)
                inverse = 1.0 / (
                    jnp.sum(e_own, axis=1, keepdims=True) + jnp.sum(e_far, axis=1, keepdims=True)
                )
                mixed += project(
                    (e_own * inverse).astype(BF16), only(own[:, pad : pad + width], lanes, head)
                )
                mixed += project(
                    (e_far * inverse).astype(BF16), only(far[:, pad : pad + width], lanes, head)
                )
            mixed = mixed.astype(BF16)
            for b in range(group):
                for k in range(near):
                    t = (first + b) ^ k
                    if t < peers:
                        outs[k][t * n_own : (t + 1) * n_own, :] = mixed[
                            b * n_own : (b + 1) * n_own
                        ]

    outs = [shape((peers * n_own, width), BF16)] * near
    return call(body, outs, [qv, kv_own, kv_far], 8 * half * n_tok * width * 2)


def spread(stats, heads):
    rows = stats.shape[0]
    return jnp.concatenate(
        [jnp.broadcast_to(stats[:, h : h + 1], (rows, HEAD_DIM)) for h in range(heads)], 1
    )


def weighted(parts, stats, heads):
    peak = functools.reduce(jnp.maximum, stats)
    weights = [jnp.exp2(s - peak) for s in stats]
    total = sum(weights)
    mixed = sum(a * spread(w / total, heads) for a, w in zip(parts, weights))
    return mixed, peak + jnp.log2(total)


def join_members(parts, where, near, share, width):
    lat_own = parts[0].shape[0]
    pad = parts[0].shape[1] - LANES
    heads = width // HEAD_DIM

    def body(*refs):
        pos, ins, out = refs[0], refs[1:-1], refs[-1]
        for k in range(near):
            rows = slice(k * share, (k + 1) * share)
            packed = [p[rows, pad:].astype(F32) for p in ins]
            stats = [s + pltpu.roll(s, LANES - 32, 1) + pltpu.roll(s, LANES - 64, 1) for s in packed]
            mixed, _ = weighted([p[rows, :width].astype(F32) for p in ins], stats, heads)
            out[pl.ds(aligned(pos[0] ^ k, share), share), :] = mixed

    return call(body, [shape((lat_own, width), F32)], [where, *parts], 0)[0]


def latents_part(near_avg, lat_cols, own, far, where, n_share):
    near, n_z = len(near_avg), len(own)
    lat_own, width = near_avg[0].shape
    slab = own[0].shape[0] - 2 * n_share
    features = near * width

    def body(*refs):
        pos, avgs, lat = refs[0], refs[1 : 1 + near], refs[1 + near]
        own_w, far_w = refs[2 + near : 2 + near + n_z], refs[2 + near + n_z : 2 + near + 2 * n_z]
        out, w_all = refs[-2:]
        w_rows = near * slab
        for core, pieces in enumerate((own_w, far_w)):
            for j, piece in enumerate(pieces):
                for i in range(near):
                    to = aligned(pos[1] ^ (2 * j + core), w_rows) + i * slab
                    w_all[pl.ds(to, slab), :] = piece[
                        2 * n_share :, i * width : (i + 1) * width
                    ].astype(F32)
        values = [a[...] for a in avgs]
        square = sum(jnp.sum(a * a, axis=1, keepdims=True) for a in values)
        rate = lax.rsqrt(square * (1.0 / features) + NORM_EPS)
        total = lat[...].astype(F32)
        for k in range(near):
            total += project(
                (values[k] * rate).astype(BF16),
                w_all[pl.ds(aligned(pos[0] ^ k, width), width), :].astype(BF16),
            )
        out[...] = total.astype(BF16)

    return call(
        body,
        [shape((lat_own, width), BF16)],
        [where, *near_avg, lat_cols, *own, *far],
        2 * lat_own * features * width,
        [pltpu.VMEM((features, width), F32)],
    )[0]


def token_mlp(parts, tok_near, w_out, gain, own, far, where, n_share):
    near, peers, n_ff = len(parts), len(tok_near), len(own) + len(far)
    width = parts[0].shape[1]
    n_own, features = tok_near[0].shape

    def body(*refs):
        pos, w_ref, gain_ref = refs[:3]
        ins = refs[3 : 3 + near]
        toks = refs[3 + near : 3 + near + peers]
        ff = refs[3 + near + peers : 3 + near + peers + n_ff]
        own_out, sends = refs[3 + near + peers + n_ff], refs[4 + near + peers + n_ff : -2]
        up_t, down = refs[-2:]
        for i, piece in enumerate(ff):
            rows = slice(i * n_share, (i + 1) * n_share)
            up_t[rows, :] = piece[:n_share, :]
            down[rows, :] = piece[n_share : 2 * n_share, :]
        group = 2 if peers % 2 == 0 else 1
        for t in range(0, peers, group):
            rows = slice(t * n_own, (t + group) * n_own)
            mid = jnp.concatenate([toks[t + b][...].astype(F32) for b in range(group)], 0)
            for k in range(near):
                mid += project(
                    ins[k][rows, :], w_ref[pl.ds(aligned(pos[0] ^ k, width), width), :]
                )
            mlp_in = (normalize(mid) * gain_ref[...]).astype(BF16)
            hidden = project_t(mlp_in, up_t[...])
            hidden = (hidden * (0.5 + 0.5 * lax.erf(hidden * (0.5**0.5)))).astype(BF16)
            partial = project(hidden, down[...])
            for b in range(group):
                rows = slice(b * n_own, (b + 1) * n_own)
                if t + b == 0:
                    own_out[...] = mid[rows] + partial[rows]
                else:
                    sends[t + b - 1][...] = partial[rows].astype(BF16)

    ff_rows = n_ff * n_share
    return call(
        body,
        [shape((n_own, features), F32)] + [shape((n_own, features), BF16)] * (peers - 1),
        [where, w_out, gain.reshape(1, -1), *parts, *tok_near, *own, *far],
        2 * peers * n_own * features * (features + 2 * ff_rows),
        [pltpu.VMEM((ff_rows, features), BF16)] * 2,
    )


def finish(own, received, lat_parts, where):
    rows, width = lat_parts[0].shape
    n_in = 1 + len(received)
    near = len(lat_parts)
    lat_shape = shape((rows, near * width), BF16)
    if width % LANES:
        order = jnp.arange(near) ^ where[0]
        placed = jnp.transpose(jnp.take(jnp.stack(lat_parts), order, axis=0), (1, 0, 2))
        total = own + sum(r.astype(F32) for r in received)
        return total.astype(BF16), placed.reshape(lat_shape.shape)

    def body(*refs):
        pos, ins, parts = refs[0], refs[1 : 1 + n_in], refs[1 + n_in : -2]
        for k, part in enumerate(parts):
            refs[-1][:, pl.ds(aligned(pos[0] ^ k, width), width)] = part[...]
        refs[-2][...] = sum(r[...].astype(F32) for r in ins).astype(BF16)

    outs = [shape(own.shape, BF16), lat_shape]
    return call(body, outs, [where, own, *received, *lat_parts], 0)


def per_device(
    tokens,
    latents,
    tok_gain,
    lat_gain,
    mlp_gain,
    w_ref_tok,
    w_val_tok,
    w_out_tok,
    w_ref_lat,
    w_val_lat,
    w_out_lat,
    w_up,
    w_down,
):
    n_group, n_member = lax.axis_size("group"), lax.axis_size("member")
    n_z = n_member // 2
    g, m = lax.axis_index("group"), lax.axis_index("member")
    where = jnp.stack([g, m]).astype(jnp.int32)
    n_own, features = tokens.shape
    lat_own = latents.shape[0]
    width, share = features // n_group, lat_own // n_group
    ff_share = w_up.shape[1] // n_group
    peers = min(n_group, MLP_PEERS)

    tok_near = gathered(tokens, "group", 1)
    lat_part, w_mine, ff_mine = prepare(
        latents, lat_gain, w_ref_lat, w_val_lat, w_out_lat, w_up, w_down, where
    )
    lat_col = gathered(lat_part, "member", 2)
    w_own = gathered(w_mine, "member", 2)
    lat_near = gathered(stack_rows(lat_col), "group", 1)
    ff_own = gathered(ff_mine, "member", 2)
    w_far = [swap(w, "member", 1) for w in w_own]
    ff_far = [swap(f, "member", 1) for f in ff_own]
    extra = [swap(f, "group", k) for k in range(peers, n_group, peers) for f in ff_own]
    extra_far = [swap(f, "member", 1) for f in extra]

    qv = queries(tok_near, tok_gain, w_ref_tok, w_val_tok, where, width)
    qv_far = swap(qv, "member", 1)
    kv_own = keys(lat_near, w_own, w_far, where)
    kv_far = swap(kv_own, "member", 1)

    row_parts = rows_part(qv, kv_own, kv_far, width, n_own, peers)
    row_parts = [row_parts[0]] + [swap(row_parts[k], "group", k) for k in range(1, n_group)]
    pieces = columns(qv, qv_far, kv_own, n_group, n_z, share, width)
    pieces = [pieces[0]] + [swap(pieces[j], "member", 2 * j) for j in range(1, n_z)]
    own_avg = join_members(pieces, where, n_group, share, width)
    avg_near = gathered(own_avg, "group", 1)
    mid, *sends = token_mlp(
        row_parts,
        tok_near[:peers],
        w_out_tok,
        mlp_gain,
        ff_own + extra,
        ff_far + extra_far,
        where,
        ff_share,
    )
    received = [swap(s, "group", k + 1) for k, s in enumerate(sends)]
    lat_cols = from_group(latents, where, width, 1)
    lat_new = latents_part(avg_near, lat_cols, ff_own, ff_far, where, ff_share)
    lat_parts = gathered(lat_new, "group", 1)
    return tuple(finish(mid, received, lat_parts, where))


def solution(mesh):
    in_specs = (
        P(("group", "member"), None),
        P("member", None),
        P(),
        P(),
        P(),
        P(),
        P(),
        P(),
        P("member", None),
        P("member", None),
        P("member", None),
        P(None, "member"),
        P("member", None),
    )
    out_specs = (P(("group", "member"), None), P("member", None))

    return jax.shard_map(per_device, mesh=mesh, in_specs=in_specs, out_specs=out_specs, check_vma=False)
```

```python
import functools

import jax
import jax.numpy as jnp
from jax import lax
from jax.experimental import pallas as pl
from jax.experimental.pallas import tpu as pltpu
from jax.sharding import PartitionSpec as P


HEAD_DIM = 64
NORM_EPS = 1e-06
LOG2E = 1.4426950408889634
RATE = HEAD_DIM ** (-0.5) * LOG2E
LANES = 128
MLP_PEERS = 4
BF16 = jnp.bfloat16
F32 = jnp.float32
AVERAGE = BF16


VMEM = pl.BlockSpec(memory_space=pltpu.VMEM)
HBM = pl.BlockSpec(memory_space=pltpu.HBM)


def normalize(values):
    return values * lax.rsqrt(jnp.mean(values * values, axis=-1, keepdims=True) + NORM_EPS)


def project(left_side, right_side):
    return jnp.dot(left_side, right_side, preferred_element_type=F32)


def project_t(left_side, right_side):
    return lax.dot_general(
        left_side, right_side, (((1,), (1,)), ((), ())), preferred_element_type=F32
    )


def swap(x, axis, offset):
    size = lax.axis_size(axis)
    return lax.ppermute(x, axis, [(i, i ^ offset) for i in range(size)])


def gathered(x, axis, step):
    size = lax.axis_size(axis)
    return [x] + [swap(x, axis, k) for k in range(step, size, step)]


def call(body, outs, ins, flops, scratch=(), left=(), grant=48 * 1024 * 1024):
    moved = sum(x.size * x.dtype.itemsize for x in ins) + sum(
        o.size * o.dtype.itemsize for o in outs
    )
    return pl.pallas_call(
        body,
        out_shape=outs,
        in_specs=[HBM if i in left else VMEM for i in range(len(ins))],
        out_specs=[VMEM] * len(outs),
        scratch_shapes=list(scratch),
        compiler_params=pltpu.CompilerParams(vmem_limit_bytes=grant),
        cost_estimate=pl.CostEstimate(flops=flops, bytes_accessed=moved, transcendentals=0),
    )(*ins)


def aligned(index, multiple):
    return pl.multiple_of(index * multiple, multiple)


def shape(dims, dtype):
    return jax.ShapeDtypeStruct(dims, dtype)


def head_lanes(width):
    return lax.broadcasted_iota(jnp.int32, (1, width), 1) // HEAD_DIM


def only(values, lanes, head):
    return jnp.where(lanes == head, values, jnp.zeros_like(values))


def side_by_side(pair, width):
    pad = ((0, 0), (0, -width % LANES))
    return jnp.concatenate([jnp.pad(w, pad) for w in pair], 1)


def from_group(x, size, dim):
    return lax.dynamic_slice_in_dim(x, lax.axis_index("group") * size, size, dim)


def queries(tok_near, gain, w_ref, width):
    near = len(tok_near)
    n_own, features = tok_near[0].shape
    if width % LANES:
        normed = (normalize(jnp.concatenate(tok_near, 0).astype(F32)) * gain).astype(BF16)
        return project(normed, from_group(w_ref, width, 1)).astype(BF16), normed

    def body(*refs):
        gain_ref, ref_w, out, normed = refs[near:]
        for k in range(near):
            rows = slice(k * n_own, (k + 1) * n_own)
            normed[rows, :] = (normalize(refs[k][...].astype(F32)) * gain_ref[...]).astype(BF16)
        cols = pl.ds(aligned(lax.axis_index("group"), width), width)
        out[...] = project(normed[...], ref_w[:, cols]).astype(BF16)

    return call(
        body,
        [shape((near * n_own, width), BF16), shape((near * n_own, features), BF16)],
        [*tok_near, gain.reshape(1, -1), w_ref],
        2 * near * n_own * features * width,
    )


def values(normed, w_val, width):
    rows, features = normed.shape
    if width % LANES:
        return project(normed, from_group(w_val, width, 1)).astype(BF16)

    def body(normed_ref, val_w, out):
        cols = pl.ds(aligned(lax.axis_index("group"), width), width)
        out[...] = project(normed_ref[...], val_w[:, cols]).astype(BF16)

    outs = [shape((rows, width), BF16)]
    return call(body, outs, [normed, w_val], 2 * rows * features * width)[0]


def prepare(latents, gain, w_ref, w_val, w_out, w_up, w_down):
    n_group = lax.axis_size("group")
    rows, features = latents.shape
    share, width = rows // n_group, features // n_group
    ff = w_up.shape[1] // n_group
    w_rows = w_ref.shape[0]
    if width % LANES or share % 16 or ff % 16 or LANES % ff:
        lat = normalize(from_group(latents, share, 0).astype(F32)) * gain
        return (
            lat.astype(BF16),
            side_by_side([from_group(w, width, 1) for w in (w_ref, w_val)], width),
            from_group(w_out, width, 1),
            jnp.concatenate([jnp.transpose(from_group(w_up, ff, 1)), from_group(w_down, ff, 0)], 0),
        )

    def body(*refs):
        lat_in, gain_in, ref_w, val_w, out_w, up_w, down_w, lat, cols, out_cols, rest = refs[:11]
        lat_rows, up_cols, turned, sems = refs[11:]
        g = lax.axis_index("group")
        mine = pl.ds(aligned(g, width), width)
        pairs = [
            (lat_in.at[pl.ds(aligned(g, share), share), :], lat_rows),
            (up_w.at[:, pl.ds(aligned(g // (LANES // ff), LANES), LANES)], up_cols),
            (ref_w.at[:, mine], cols.at[:, :width]),
            (val_w.at[:, mine], cols.at[:, width:]),
            (out_w.at[:, mine], out_cols),
            (down_w.at[pl.ds(aligned(g, ff), ff), :], rest.at[ff:, :]),
        ]
        copies = [
            pltpu.make_async_copy(source, to, sems.at[i]) for i, (source, to) in enumerate(pairs)
        ]
        for copy in copies:
            copy.start()
        copies[0].wait()
        lat[...] = (normalize(lat_rows[...].astype(F32)) * gain_in[...]).astype(BF16)
        copies[1].wait()
        turned[...] = jnp.transpose(up_cols[...].astype(F32))
        first = aligned(lax.rem(g, LANES // ff), ff)
        rest[:ff, :] = turned[pl.ds(first, ff), :].astype(BF16)
        for copy in copies[2:]:
            copy.wait()

    outs = ((share, features), (w_rows, 2 * width), (w_rows, width), (2 * ff, features))
    return call(
        body,
        [shape(o, BF16) for o in outs],
        [latents, gain.reshape(1, -1), w_ref, w_val, w_out, w_up, w_down],
        0,
        [
            pltpu.VMEM((share, features), BF16),
            pltpu.VMEM((features, LANES), BF16),
            pltpu.VMEM((LANES, features), F32),
            pltpu.SemaphoreType.DMA((6,)),
        ],
        left=(0, 2, 3, 4, 5, 6),
        grant=None,
    )


def stack_rows(parts):
    rows, cols = parts[0].shape

    def body(*refs):
        for k, part in enumerate(refs[:-1]):
            refs[-1][k * rows : (k + 1) * rows, :] = part[...]

    return call(body, [shape((len(parts) * rows, cols), parts[0].dtype)], parts, 0)[0]


def keys(lat_near, w_own, w_far):
    near, n_z = len(lat_near), len(w_own)
    rows, features = lat_near[0].shape
    w_rows, cols = w_own[0].shape

    def body(*refs):
        lats = refs[:near]
        own, far = refs[near : near + n_z], refs[near + n_z : near + 2 * n_z]
        m = lax.axis_index("member")
        out, w_all, lat_all = refs[-3:]
        for core, pieces in enumerate((own, far)):
            for j, piece in enumerate(pieces):
                w_all[pl.ds(aligned(m ^ (2 * j + core), w_rows), w_rows), :] = piece[...]
        for k in range(near):
            lat_all[k * rows : (k + 1) * rows, :] = lats[k][...]
        out[...] = project(lat_all[...], w_all[...]).astype(BF16)

    return call(
        body,
        [shape((near * rows, cols), BF16)],
        [*lat_near, *w_own, *w_far],
        2 * near * rows * features * cols,
        [pltpu.VMEM((features, cols), BF16), pltpu.VMEM((near * rows, features), BF16)],
    )[0]


def columns(q_own, q_far, v_own, v_far, kv_own, near, n_z, share, width):
    n_tok, pad = q_own.shape[0], kv_own.shape[1] // 2
    heads = width // HEAD_DIM
    block = n_z * share
    group = 2 if near % 2 == 0 else 1
    step = group * block

    def body(own, far, own_v, far_v, k_ref, *outs):
        lanes = head_lanes(width)
        stat_lanes = lax.broadcasted_iota(jnp.int32, (1, LANES), 1)
        for first in range(0, near, group):
            k_rows = k_ref[first * block : first * block + step, :width]
            mixed = jnp.zeros((step, width), F32)
            scale = jnp.zeros((step, width), F32)
            stats = jnp.zeros((step, LANES), F32)
            for head in range(heads):
                k_head = only(k_rows, lanes, head)
                scores = [project_t(k_head, q[...]) for q in (own, far)]
                peak = jnp.maximum(*[jnp.max(s, axis=1, keepdims=True) for s in scores])
                powers = [jnp.exp2((s - peak) * RATE) for s in scores]
                total = sum(jnp.sum(e, axis=1, keepdims=True) for e in powers)
                for e, v in zip(powers, (own_v, far_v)):
                    mixed += project(e.astype(BF16), only(v[...], lanes, head))
                scale = jnp.where(lanes == head, 1.0 / total, scale)
                stats = jnp.where(stat_lanes == head, peak * RATE + jnp.log2(total), stats)
            mixed = (mixed * scale).astype(BF16)
            high = stats.astype(BF16).astype(F32)
            middle = (stats - high).astype(BF16).astype(F32)
            low = stats - high - middle
            packed = high + pltpu.roll(middle, 32, 1) + pltpu.roll(low, 64, 1)
            packed = packed.astype(BF16)
            for k in range(group):
                for j in range(n_z):
                    rows = slice(k * block + j * share, k * block + (j + 1) * share)
                    to = slice((first + k) * share, (first + k + 1) * share)
                    outs[j][to, :width] = mixed[rows]
                    if width < pad:
                        outs[j][to, width:pad] = jnp.zeros((share, pad - width), BF16)
                    outs[j][to, pad:] = packed[rows]

    outs = [shape((near * share, pad + LANES), BF16)] * n_z
    flops = 16 * near * block * n_tok * width
    return call(body, outs, [q_own, q_far, v_own, v_far, kv_own], flops)


def rows_part(q, kv_own, kv_far, n_own, peers):
    n_tok, width = q.shape
    half, pad2 = kv_own.shape
    pad = pad2 // 2
    heads = width // HEAD_DIM
    near = n_tok // n_own

    def body(q_ref, own, far, *outs):
        lanes = head_lanes(width)
        group = 2 if near % 2 == 0 else 1
        for first in range(0, near, group):
            q_rows = q_ref[first * n_own : (first + group) * n_own, :]
            mixed = jnp.zeros((group * n_own, width), F32)
            for head in range(heads):
                q_head = only(q_rows, lanes, head)
                s_own = project_t(q_head, own[:, :width])
                s_far = project_t(q_head, far[:, :width])
                peak = jnp.maximum(
                    jnp.max(s_own, axis=1, keepdims=True), jnp.max(s_far, axis=1, keepdims=True)
                )
                e_own = jnp.exp2((s_own - peak) * RATE)
                e_far = jnp.exp2((s_far - peak) * RATE)
                inverse = 1.0 / (
                    jnp.sum(e_own, axis=1, keepdims=True) + jnp.sum(e_far, axis=1, keepdims=True)
                )
                mixed += project(
                    (e_own * inverse).astype(BF16), only(own[:, pad : pad + width], lanes, head)
                )
                mixed += project(
                    (e_far * inverse).astype(BF16), only(far[:, pad : pad + width], lanes, head)
                )
            mixed = mixed.astype(BF16)
            for b in range(group):
                for k in range(near):
                    t = (first + b) ^ k
                    if t < peers:
                        outs[k][t * n_own : (t + 1) * n_own, :] = mixed[
                            b * n_own : (b + 1) * n_own
                        ]

    outs = [shape((peers * n_own, width), BF16)] * near
    return call(body, outs, [q, kv_own, kv_far], 8 * half * n_tok * width * 2)


def spread(stats, heads):
    rows = stats.shape[0]
    return jnp.concatenate(
        [jnp.broadcast_to(stats[:, h : h + 1], (rows, HEAD_DIM)) for h in range(heads)], 1
    )


def weighted(parts, stats, heads):
    peak = functools.reduce(jnp.maximum, stats)
    weights = [jnp.exp2(s - peak) for s in stats]
    total = sum(weights)
    inverse = 1.0 / total
    mixed = sum(a * spread(w * inverse, heads) for a, w in zip(parts, weights))
    return mixed


def join_members(parts, near, share, width):
    lat_own = parts[0].shape[0]
    pad = parts[0].shape[1] - LANES
    heads = width // HEAD_DIM

    def body(*refs):
        ins, out = refs[:-1], refs[-1]
        g = lax.axis_index("group")
        packed = [p[:, pad:].astype(F32) for p in ins]
        stats = [s + pltpu.roll(s, LANES - 32, 1) + pltpu.roll(s, LANES - 64, 1) for s in packed]
        mixed = weighted([p[:, :width].astype(F32) for p in ins], stats, heads)
        for k in range(near):
            first = k * share if share % 16 else aligned(g ^ k, share)
            out[pl.ds(first, share), :] = mixed[k * share : (k + 1) * share].astype(out.dtype)

    joined = call(body, [shape((lat_own, width), AVERAGE)], parts, 0)[0]
    if share % 16:
        order = jnp.arange(near) ^ lax.axis_index("group")
        blocks = jnp.take(joined.reshape(near, share, width), order, axis=0)
        joined = blocks.reshape(lat_own, width)
    return joined


def latents_part(near_avg, lat_cols, own, far):
    near, n_z = len(near_avg), len(own)
    lat_own, width = near_avg[0].shape
    w_rows = own[0].shape[0]
    features = near * width

    def body(*refs):
        avgs, lat = refs[:near], refs[near]
        own_w, far_w = refs[1 + near : 1 + near + n_z], refs[1 + near + n_z : 1 + near + 2 * n_z]
        g, m = lax.axis_index("group"), lax.axis_index("member")
        out, w_all = refs[-2:]
        for core, pieces in enumerate((own_w, far_w)):
            for j, piece in enumerate(pieces):
                to = aligned(m ^ (2 * j + core), w_rows)
                w_all[pl.ds(to, w_rows), :] = piece[...].astype(F32)
        values = [a[...].astype(F32) for a in avgs]
        square = sum(jnp.sum(a * a, axis=1, keepdims=True) for a in values)
        rate = lax.rsqrt(square * (1.0 / features) + NORM_EPS)
        if width % LANES == 0:
            total = lat[:, pl.ds(aligned(g, width), width)].astype(F32)
        else:
            total = lat[...].astype(F32)
        for k in range(near):
            total += project(
                (values[k] * rate).astype(BF16),
                w_all[pl.ds(aligned(g ^ k, width), width), :].astype(BF16),
            )
        out[...] = total.astype(BF16)

    return call(
        body,
        [shape((lat_own, width), BF16)],
        [*near_avg, lat_cols, *own, *far],
        2 * lat_own * features * width,
        [pltpu.VMEM((features, width), F32)],
    )[0]


def token_mlp(parts, tok_near, w_out, gain, own, far, n_share):
    near, peers, n_ff = len(parts), len(tok_near), len(own) + len(far)
    width = parts[0].shape[1]
    n_own, features = tok_near[0].shape

    def body(*refs):
        g = lax.axis_index("group")
        w_ref, gain_ref = refs[:2]
        ins = refs[2 : 2 + near]
        toks = refs[2 + near : 2 + near + peers]
        ff = refs[2 + near + peers : 2 + near + peers + n_ff]
        own_out, sends = refs[2 + near + peers + n_ff], refs[3 + near + peers + n_ff : -2]
        up_t, down = refs[-2:]
        for i, piece in enumerate(ff):
            rows = slice(i * n_share, (i + 1) * n_share)
            up_t[rows, :] = piece[:n_share, :]
            down[rows, :] = piece[n_share : 2 * n_share, :]
        group = 2 if peers % 2 == 0 else 1
        for t in range(0, peers, group):
            rows = slice(t * n_own, (t + group) * n_own)
            mid = jnp.concatenate([toks[t + b][...].astype(F32) for b in range(group)], 0)
            for k in range(near):
                mid += project(
                    ins[k][rows, :], w_ref[pl.ds(aligned(g ^ k, width), width), :]
                )
            mlp_in = (normalize(mid) * gain_ref[...]).astype(BF16)
            hidden = project_t(mlp_in, up_t[...])
            hidden = (hidden * (0.5 + 0.5 * lax.erf(hidden * (0.5**0.5)))).astype(BF16)
            partial = project(hidden, down[...])
            for b in range(group):
                rows = slice(b * n_own, (b + 1) * n_own)
                if t + b == 0:
                    own_out[...] = mid[rows] + partial[rows]
                else:
                    sends[t + b - 1][...] = partial[rows].astype(BF16)

    ff_rows = n_ff * n_share
    return call(
        body,
        [shape((n_own, features), F32)] + [shape((n_own, features), BF16)] * (peers - 1),
        [w_out, gain.reshape(1, -1), *parts, *tok_near, *own, *far],
        2 * peers * n_own * features * (features + 2 * ff_rows),
        [pltpu.VMEM((ff_rows, features), BF16)] * 2,
    )


def add_up(own, received):
    def body(*refs):
        refs[-1][...] = sum(r[...].astype(F32) for r in refs[:-1]).astype(BF16)

    return call(body, [shape(own.shape, BF16)], [own, *received], 0)[0]


def place_columns(parts):
    rows, width = parts[0].shape
    near = len(parts)
    if width % LANES:
        order = jnp.arange(near) ^ lax.axis_index("group")
        placed = jnp.transpose(jnp.take(jnp.stack(parts), order, axis=0), (1, 0, 2))
        return placed.reshape(rows, near * width)

    def body(*refs):
        g = lax.axis_index("group")
        for k, part in enumerate(refs[:-1]):
            refs[-1][:, pl.ds(aligned(g ^ k, width), width)] = part[...]

    outs = [shape((rows, near * width), BF16)]
    return call(body, outs, parts, 0)[0]


def per_device(
    tokens,
    latents,
    tok_gain,
    lat_gain,
    mlp_gain,
    w_ref_tok,
    w_val_tok,
    w_out_tok,
    w_ref_lat,
    w_val_lat,
    w_out_lat,
    w_up,
    w_down,
):
    n_group, n_member = lax.axis_size("group"), lax.axis_size("member")
    n_z = n_member // 2
    n_own, features = tokens.shape
    lat_own = latents.shape[0]
    width, share = features // n_group, lat_own // n_group
    ff_share = w_up.shape[1] // n_group
    peers = min(n_group, MLP_PEERS)

    tok_near = gathered(tokens, "group", 1)
    lat_part, w_mine, out_mine, ff_mine = prepare(
        latents, lat_gain, w_ref_lat, w_val_lat, w_out_lat, w_up, w_down
    )
    lat_col = gathered(lat_part, "member", 2)
    w_own = gathered(w_mine, "member", 2)
    lat_near = gathered(stack_rows(lat_col), "group", 1)
    ff_own = gathered(ff_mine, "member", 2)
    out_own = gathered(out_mine, "member", 2)
    out_far = [swap(w, "member", 1) for w in out_own]
    w_far = [swap(w, "member", 1) for w in w_own]
    ff_far = [swap(f, "member", 1) for f in ff_own]
    extra = [swap(f, "group", k) for k in range(peers, n_group, peers) for f in ff_own]
    extra_far = [swap(f, "member", 1) for f in extra]

    q, normed = queries(tok_near, tok_gain, w_ref_tok, width)
    kv_own = keys(lat_near, w_own, w_far)
    kv_far = swap(kv_own, "member", 1)
    v = values(normed, w_val_tok, width)
    q_far, v_far = swap(q, "member", 1), swap(v, "member", 1)

    row_parts = rows_part(q, kv_own, kv_far, n_own, peers)
    row_parts = [row_parts[0]] + [swap(row_parts[k], "group", k) for k in range(1, n_group)]
    pieces = columns(q, q_far, v, v_far, kv_own, n_group, n_z, share, width)
    pieces = [pieces[0]] + [swap(pieces[j], "member", 2 * j) for j in range(1, n_z)]
    own_avg = join_members(pieces, n_group, share, width)
    avg_near = gathered(own_avg, "group", 1)
    mid, *sends = token_mlp(
        row_parts,
        tok_near[:peers],
        w_out_tok,
        mlp_gain,
        ff_own + extra,
        ff_far + extra_far,
        ff_share,
    )
    received = [swap(s, "group", k + 1) for k, s in enumerate(sends)]
    lat_cols = latents if width % LANES == 0 else from_group(latents, width, 1)
    lat_new = latents_part(avg_near, lat_cols, out_own, out_far)
    lat_parts = gathered(lat_new, "group", 1)
    return add_up(mid, received), place_columns(lat_parts)


def solution(mesh):
    in_specs = (
        P(("group", "member"), None),
        P("member", None),
        P(),
        P(),
        P(),
        P(),
        P(),
        P(),
        P("member", None),
        P("member", None),
        P("member", None),
        P(None, "member"),
        P("member", None),
    )
    out_specs = (P(("group", "member"), None), P("member", None))

    return jax.shard_map(per_device, mesh=mesh, in_specs=in_specs, out_specs=out_specs, check_vma=False)
```

```python
import functools

import jax
import jax.numpy as jnp
from jax import lax
from jax.experimental import pallas as pl
from jax.experimental.pallas import tpu as pltpu
from jax.sharding import PartitionSpec as P


HEAD_DIM = 64
NORM_EPS = 1e-06
LOG2E = 1.4426950408889634
RATE = HEAD_DIM ** (-0.5) * LOG2E
LANES = 128
MLP_PEERS = 4
BF16 = jnp.bfloat16
F32 = jnp.float32
AVERAGE = BF16


VMEM = pl.BlockSpec(memory_space=pltpu.VMEM)
HBM = pl.BlockSpec(memory_space=pltpu.HBM)


def normalize(values):
    return values * lax.rsqrt(jnp.mean(values * values, axis=-1, keepdims=True) + NORM_EPS)


def project(left_side, right_side):
    return jnp.dot(left_side, right_side, preferred_element_type=F32)


def project_t(left_side, right_side):
    return lax.dot_general(
        left_side, right_side, (((1,), (1,)), ((), ())), preferred_element_type=F32
    )


def swap(x, axis, offset):
    size = lax.axis_size(axis)
    return lax.ppermute(x, axis, [(i, i ^ offset) for i in range(size)])


def exchange(axis, step, sends):
    results = []
    for i, x in enumerate(sends):
        results.append(swap(x, axis, step * (i + 1)))
    return results


def gathered(x, axis, step):
    return [x] + exchange(axis, step, [x] * (lax.axis_size(axis) // step - 1))


def relayed(x):
    n_z = lax.axis_size("member") // 2
    pieces = {0: x}
    hop = n_z // 2
    while hop:
        for j in sorted(pieces):
            pieces[j + hop] = swap(pieces[j], "member", 2 * hop)
        hop //= 2
    return [pieces[j] for j in range(n_z)]


def call(body, outs, ins, flops, scratch=(), left=(), grant=48 * 1024 * 1024):
    moved = sum(x.size * x.dtype.itemsize for x in ins) + sum(
        o.size * o.dtype.itemsize for o in outs
    )
    return pl.pallas_call(
        body,
        out_shape=outs,
        in_specs=[HBM if i in left else VMEM for i in range(len(ins))],
        out_specs=[VMEM] * len(outs),
        scratch_shapes=list(scratch),
        compiler_params=pltpu.CompilerParams(vmem_limit_bytes=grant),
        cost_estimate=pl.CostEstimate(flops=flops, bytes_accessed=moved, transcendentals=0),
    )(*ins)


def aligned(index, multiple):
    return pl.multiple_of(index * multiple, multiple)


def shape(dims, dtype):
    return jax.ShapeDtypeStruct(dims, dtype)


def head_lanes(width):
    return lax.broadcasted_iota(jnp.int32, (1, width), 1) // HEAD_DIM


def only(values, lanes, head):
    return jnp.where(lanes == head, values, jnp.zeros_like(values))


def side_by_side(pair, width):
    pad = ((0, 0), (0, -width % LANES))
    return jnp.concatenate([jnp.pad(w, pad) for w in pair], 1)


def from_group(x, size, dim):
    return lax.dynamic_slice_in_dim(x, lax.axis_index("group") * size, size, dim)


def queries(tok_near, gain, w_ref, width):
    near = len(tok_near)
    n_own, features = tok_near[0].shape
    if width % LANES:
        normed = (normalize(jnp.concatenate(tok_near, 0).astype(F32)) * gain).astype(BF16)
        return project(normed, from_group(w_ref, width, 1)).astype(BF16), normed

    def body(*refs):
        gain_ref, ref_w, out, normed = refs[near:]
        for k in range(near):
            rows = slice(k * n_own, (k + 1) * n_own)
            normed[rows, :] = (normalize(refs[k][...].astype(F32)) * gain_ref[...]).astype(BF16)
        cols = pl.ds(aligned(lax.axis_index("group"), width), width)
        out[...] = project(normed[...], ref_w[:, cols]).astype(BF16)

    return call(
        body,
        [shape((near * n_own, width), BF16), shape((near * n_own, features), BF16)],
        [*tok_near, gain.reshape(1, -1), w_ref],
        2 * near * n_own * features * width,
    )


def values(normed, w_val, width):
    rows, features = normed.shape
    if width % LANES:
        return project(normed, from_group(w_val, width, 1)).astype(BF16)

    def body(normed_ref, val_w, out):
        cols = pl.ds(aligned(lax.axis_index("group"), width), width)
        out[...] = project(normed_ref[...], val_w[:, cols]).astype(BF16)

    outs = [shape((rows, width), BF16)]
    return call(body, outs, [normed, w_val], 2 * rows * features * width)[0]


def latents_norm(latents, gain):
    rows, features = latents.shape
    share = rows // lax.axis_size("group")
    if share % 16:
        lat = normalize(from_group(latents, share, 0).astype(F32)) * gain
        return lat.astype(BF16)

    def body(lat_in, gain_in, out, lat_rows, gain_row, sems):
        rows = pl.ds(aligned(lax.axis_index("group"), share), share)
        copies = [
            pltpu.make_async_copy(lat_in.at[rows, :], lat_rows, sems.at[0]),
            pltpu.make_async_copy(gain_in, gain_row, sems.at[1]),
        ]
        for copy in copies:
            copy.start()
        for copy in copies:
            copy.wait()
        out[...] = (normalize(lat_rows[...].astype(F32)) * gain_row[...]).astype(BF16)

    return call(
        body,
        [shape((share, features), BF16)],
        [latents, gain.reshape(1, -1)],
        0,
        [
            pltpu.VMEM((share, features), BF16),
            pltpu.VMEM((1, features), F32),
            pltpu.SemaphoreType.DMA((2,)),
        ],
        left=(0, 1),
        grant=None,
    )[0]


def prepare(w_ref, w_val, w_out, w_up, w_down):
    n_group = lax.axis_size("group")
    features = w_ref.shape[1]
    width = features // n_group
    ff = w_up.shape[1] // n_group
    w_rows = w_ref.shape[0]
    slab = w_rows // n_group
    if width % LANES or slab % 16 or ff % 16 or LANES % ff:
        out_cols = from_group(w_out, width, 1)
        return (
            side_by_side([from_group(w, width, 1) for w in (w_ref, w_val)], width),
            jnp.concatenate(
                [
                    jnp.transpose(from_group(w_up, ff, 1)),
                    from_group(w_down, ff, 0),
                    jnp.concatenate(
                        [out_cols[i * slab : (i + 1) * slab] for i in range(n_group)], 1
                    ),
                ],
                0,
            ),
        )

    def body(*refs):
        ref_w, val_w, out_w, up_w, down_w, cols, rest = refs[:7]
        up_cols, turned, sems = refs[7:]
        g = lax.axis_index("group")
        mine = pl.ds(aligned(g, width), width)
        pairs = [
            (up_w.at[:, pl.ds(aligned(g // (LANES // ff), LANES), LANES)], up_cols),
            (ref_w.at[:, mine], cols.at[:, :width]),
            (val_w.at[:, mine], cols.at[:, width:]),
            (down_w.at[pl.ds(aligned(g, ff), ff), :], rest.at[ff : 2 * ff, :]),
        ]
        for i in range(n_group):
            source = out_w.at[i * slab : (i + 1) * slab, mine]
            pairs.append((source, rest.at[2 * ff :, i * width : (i + 1) * width]))
        copies = [
            pltpu.make_async_copy(source, to, sems.at[i]) for i, (source, to) in enumerate(pairs)
        ]
        for copy in copies:
            copy.start()
        copies[0].wait()
        turned[...] = jnp.transpose(up_cols[...].astype(F32))
        first = aligned(lax.rem(g, LANES // ff), ff)
        rest[:ff, :] = turned[pl.ds(first, ff), :].astype(BF16)
        for copy in copies[1:]:
            copy.wait()

    outs = ((w_rows, 2 * width), (2 * ff + slab, features))
    return call(
        body,
        [shape(o, BF16) for o in outs],
        [w_ref, w_val, w_out, w_up, w_down],
        0,
        [
            pltpu.VMEM((features, LANES), BF16),
            pltpu.VMEM((LANES, features), F32),
            pltpu.SemaphoreType.DMA((4 + n_group,)),
        ],
        left=(0, 1, 2, 3, 4),
        grant=None,
    )


def stack_rows(parts):
    rows, cols = parts[0].shape

    def body(*refs):
        for k, part in enumerate(refs[:-1]):
            refs[-1][k * rows : (k + 1) * rows, :] = part[...]

    return call(body, [shape((len(parts) * rows, cols), parts[0].dtype)], parts, 0)[0]


def keys(lat_near, w_own, w_far):
    near, n_z = len(lat_near), len(w_own)
    rows, features = lat_near[0].shape
    w_rows, cols = w_own[0].shape

    def body(*refs):
        lats = refs[:near]
        own, far = refs[near : near + n_z], refs[near + n_z : near + 2 * n_z]
        m = lax.axis_index("member")
        out, w_all, lat_all = refs[-3:]
        for core, pieces in enumerate((own, far)):
            for j, piece in enumerate(pieces):
                w_all[pl.ds(aligned(m ^ (2 * j + core), w_rows), w_rows), :] = piece[...]
        for k in range(near):
            lat_all[k * rows : (k + 1) * rows, :] = lats[k][...]
        out[...] = project(lat_all[...], w_all[...]).astype(BF16)

    return call(
        body,
        [shape((near * rows, cols), BF16)],
        [*lat_near, *w_own, *w_far],
        2 * near * rows * features * cols,
        [pltpu.VMEM((features, cols), BF16), pltpu.VMEM((near * rows, features), BF16)],
    )[0]


def columns(q_own, q_far, v_own, v_far, kv_own, near, n_z, share, width):
    n_tok, pad = q_own.shape[0], kv_own.shape[1] // 2
    heads = width // HEAD_DIM
    block = n_z * share
    group = 2 if near % 2 == 0 else 1
    step = group * block

    def body(own, far, own_v, far_v, k_ref, *outs):
        lanes = head_lanes(width)
        stat_lanes = lax.broadcasted_iota(jnp.int32, (1, LANES), 1)
        for first in range(0, near, group):
            k_rows = k_ref[first * block : first * block + step, :width]
            mixed = jnp.zeros((step, width), F32)
            scale = jnp.zeros((step, width), F32)
            stats = jnp.zeros((step, LANES), F32)
            for head in range(heads):
                k_head = only(k_rows, lanes, head)
                scores = [project_t(k_head, q[...]) for q in (own, far)]
                peak = jnp.maximum(*[jnp.max(s, axis=1, keepdims=True) for s in scores])
                powers = [jnp.exp2((s - peak) * RATE) for s in scores]
                total = sum(jnp.sum(e, axis=1, keepdims=True) for e in powers)
                for e, v in zip(powers, (own_v, far_v)):
                    mixed += project(e.astype(BF16), only(v[...], lanes, head))
                scale = jnp.where(lanes == head, 1.0 / total, scale)
                stats = jnp.where(stat_lanes == head, peak * RATE + jnp.log2(total), stats)
            mixed = (mixed * scale).astype(BF16)
            high = stats.astype(BF16).astype(F32)
            middle = (stats - high).astype(BF16).astype(F32)
            low = stats - high - middle
            packed = high + pltpu.roll(middle, 32, 1) + pltpu.roll(low, 64, 1)
            packed = packed.astype(BF16)
            for k in range(group):
                for j in range(n_z):
                    rows = slice(k * block + j * share, k * block + (j + 1) * share)
                    to = slice((first + k) * share, (first + k + 1) * share)
                    outs[j][to, :width] = mixed[rows]
                    if width < pad:
                        outs[j][to, width:pad] = jnp.zeros((share, pad - width), BF16)
                    outs[j][to, pad:] = packed[rows]

    outs = [shape((near * share, pad + LANES), BF16)] * n_z
    flops = 16 * near * block * n_tok * width
    return call(body, outs, [q_own, q_far, v_own, v_far, kv_own], flops)


def rows_part(q, kv_own, kv_far, n_own, peers):
    n_tok, width = q.shape
    half, pad2 = kv_own.shape
    pad = pad2 // 2
    heads = width // HEAD_DIM
    near = n_tok // n_own

    def body(q_ref, own, far, *outs):
        lanes = head_lanes(width)
        group = 2 if near % 2 == 0 else 1
        for first in range(0, near, group):
            q_rows = q_ref[first * n_own : (first + group) * n_own, :]
            mixed = jnp.zeros((group * n_own, width), F32)
            for head in range(heads):
                q_head = only(q_rows, lanes, head)
                s_own = project_t(q_head, own[:, :width])
                s_far = project_t(q_head, far[:, :width])
                peak = jnp.maximum(
                    jnp.max(s_own, axis=1, keepdims=True), jnp.max(s_far, axis=1, keepdims=True)
                )
                e_own = jnp.exp2((s_own - peak) * RATE)
                e_far = jnp.exp2((s_far - peak) * RATE)
                inverse = 1.0 / (
                    jnp.sum(e_own, axis=1, keepdims=True) + jnp.sum(e_far, axis=1, keepdims=True)
                )
                mixed += project(
                    (e_own * inverse).astype(BF16), only(own[:, pad : pad + width], lanes, head)
                )
                mixed += project(
                    (e_far * inverse).astype(BF16), only(far[:, pad : pad + width], lanes, head)
                )
            mixed = mixed.astype(BF16)
            for b in range(group):
                for k in range(near):
                    t = (first + b) ^ k
                    if t < peers:
                        outs[k][t * n_own : (t + 1) * n_own, :] = mixed[
                            b * n_own : (b + 1) * n_own
                        ]

    outs = [shape((peers * n_own, width), BF16)] * near
    return call(body, outs, [q, kv_own, kv_far], 8 * half * n_tok * width * 2)


def spread(stats, heads):
    rows = stats.shape[0]
    return jnp.concatenate(
        [jnp.broadcast_to(stats[:, h : h + 1], (rows, HEAD_DIM)) for h in range(heads)], 1
    )


def weighted(parts, stats, heads):
    peak = functools.reduce(jnp.maximum, stats)
    weights = [jnp.exp2(s - peak) for s in stats]
    total = sum(weights)
    inverse = 1.0 / total
    mixed = sum(a * spread(w * inverse, heads) for a, w in zip(parts, weights))
    return mixed


def join_members(parts, near, share, width):
    lat_own = parts[0].shape[0]
    pad = parts[0].shape[1] - LANES
    heads = width // HEAD_DIM

    def body(*refs):
        ins, out = refs[:-1], refs[-1]
        g = lax.axis_index("group")
        packed = [p[:, pad:].astype(F32) for p in ins]
        stats = [s + pltpu.roll(s, LANES - 32, 1) + pltpu.roll(s, LANES - 64, 1) for s in packed]
        mixed = weighted([p[:, :width].astype(F32) for p in ins], stats, heads)
        for k in range(near):
            first = k * share if share % 16 else aligned(g ^ k, share)
            out[pl.ds(first, share), :] = mixed[k * share : (k + 1) * share].astype(out.dtype)

    joined = call(body, [shape((lat_own, width), AVERAGE)], parts, 0)[0]
    if share % 16:
        order = jnp.arange(near) ^ lax.axis_index("group")
        blocks = jnp.take(joined.reshape(near, share, width), order, axis=0)
        joined = blocks.reshape(lat_own, width)
    return joined


def latents_part(near_avg, lat_cols, own, far, n_share):
    near, n_z = len(near_avg), len(own)
    lat_own, width = near_avg[0].shape
    slab = own[0].shape[0] - 2 * n_share
    features = near * width

    def body(*refs):
        avgs, lat = refs[:near], refs[near]
        own_w, far_w = refs[1 + near : 1 + near + n_z], refs[1 + near + n_z : 1 + near + 2 * n_z]
        g, m = lax.axis_index("group"), lax.axis_index("member")
        out, w_all = refs[-2:]
        w_rows = near * slab
        for core, pieces in enumerate((own_w, far_w)):
            for j, piece in enumerate(pieces):
                for i in range(near):
                    to = aligned(m ^ (2 * j + core), w_rows) + i * slab
                    w_all[pl.ds(to, slab), :] = piece[
                        2 * n_share :, i * width : (i + 1) * width
                    ].astype(F32)
        values = [a[...].astype(F32) for a in avgs]
        square = sum(jnp.sum(a * a, axis=1, keepdims=True) for a in values)
        rate = lax.rsqrt(square * (1.0 / features) + NORM_EPS)
        if width % LANES == 0:
            total = lat[:, pl.ds(aligned(g, width), width)].astype(F32)
        else:
            total = lat[...].astype(F32)
        for k in range(near):
            total += project(
                (values[k] * rate).astype(BF16),
                w_all[pl.ds(aligned(g ^ k, width), width), :].astype(BF16),
            )
        out[...] = total.astype(BF16)

    return call(
        body,
        [shape((lat_own, width), BF16)],
        [*near_avg, lat_cols, *own, *far],
        2 * lat_own * features * width,
        [pltpu.VMEM((features, width), F32)],
    )[0]


def token_mlp(parts, tok_near, w_out, gain, own, far, n_share):
    near, peers, n_ff = len(parts), len(tok_near), len(own) + len(far)
    width = parts[0].shape[1]
    n_own, features = tok_near[0].shape

    def body(*refs):
        g = lax.axis_index("group")
        w_ref, gain_ref = refs[:2]
        ins = refs[2 : 2 + near]
        toks = refs[2 + near : 2 + near + peers]
        ff = refs[2 + near + peers : 2 + near + peers + n_ff]
        own_out, sends = refs[2 + near + peers + n_ff], refs[3 + near + peers + n_ff : -2]
        up_t, down = refs[-2:]
        for i, piece in enumerate(ff):
            rows = slice(i * n_share, (i + 1) * n_share)
            up_t[rows, :] = piece[:n_share, :]
            down[rows, :] = piece[n_share : 2 * n_share, :]
        group = peers
        for t in range(0, peers, group):
            rows = slice(t * n_own, (t + group) * n_own)
            mid = jnp.concatenate([toks[t + b][...].astype(F32) for b in range(group)], 0)
            for k in range(near):
                mid += project(
                    ins[k][rows, :], w_ref[pl.ds(aligned(g ^ k, width), width), :]
                )
            mlp_in = (normalize(mid) * gain_ref[...]).astype(BF16)
            hidden = project_t(mlp_in, up_t[...])
            hidden = (hidden * (0.5 + 0.5 * lax.erf(hidden * (0.5**0.5)))).astype(BF16)
            partial = project(hidden, down[...])
            for b in range(group):
                rows = slice(b * n_own, (b + 1) * n_own)
                if t + b == 0:
                    own_out[...] = mid[rows] + partial[rows]
                else:
                    sends[t + b - 1][...] = partial[rows].astype(BF16)

    ff_rows = n_ff * n_share
    return call(
        body,
        [shape((n_own, features), F32)] + [shape((n_own, features), BF16)] * (peers - 1),
        [w_out, gain.reshape(1, -1), *parts, *tok_near, *own, *far],
        2 * peers * n_own * features * (features + 2 * ff_rows),
        [pltpu.VMEM((ff_rows, features), BF16)] * 2,
    )


def add_up(own, received):
    def body(*refs):
        refs[-1][...] = sum(r[...].astype(F32) for r in refs[:-1]).astype(BF16)

    return call(body, [shape(own.shape, BF16)], [own, *received], 0)[0]


def place_columns(parts):
    rows, width = parts[0].shape
    near = len(parts)
    if width % LANES:
        order = jnp.arange(near) ^ lax.axis_index("group")
        placed = jnp.transpose(jnp.take(jnp.stack(parts), order, axis=0), (1, 0, 2))
        return placed.reshape(rows, near * width)

    def body(*refs):
        g = lax.axis_index("group")
        for k, part in enumerate(refs[:-1]):
            refs[-1][:, pl.ds(aligned(g ^ k, width), width)] = part[...]

    outs = [shape((rows, near * width), BF16)]
    return call(body, outs, parts, 0)[0]


def per_device(
    tokens,
    latents,
    tok_gain,
    lat_gain,
    mlp_gain,
    w_ref_tok,
    w_val_tok,
    w_out_tok,
    w_ref_lat,
    w_val_lat,
    w_out_lat,
    w_up,
    w_down,
):
    n_group, n_member = lax.axis_size("group"), lax.axis_size("member")
    n_z = n_member // 2
    n_own, features = tokens.shape
    lat_own = latents.shape[0]
    width, share = features // n_group, lat_own // n_group
    ff_share = w_up.shape[1] // n_group
    peers = min(n_group, MLP_PEERS)

    tok_near = gathered(tokens, "group", 1)
    lat_col = gathered(latents_norm(latents, lat_gain), "member", 2)
    w_mine, ff_mine = prepare(w_ref_lat, w_val_lat, w_out_lat, w_up, w_down)
    w_own = relayed(w_mine)
    lat_near = gathered(stack_rows(lat_col), "group", 1)
    ff_own = relayed(ff_mine)
    w_far = [swap(w, "member", 1) for w in w_own]
    ff_far = [swap(f, "member", 1) for f in ff_own]
    extra = [swap(f, "group", k) for k in range(peers, n_group, peers) for f in ff_own]
    extra_far = [swap(f, "member", 1) for f in extra]

    q, normed = queries(tok_near, tok_gain, w_ref_tok, width)
    kv_own = keys(lat_near, w_own, w_far)
    kv_far = swap(kv_own, "member", 1)
    v = values(normed, w_val_tok, width)
    q_far, v_far = swap(q, "member", 1), swap(v, "member", 1)

    row_parts = rows_part(q, kv_own, kv_far, n_own, peers)
    row_parts = [row_parts[0]] + exchange("group", 1, row_parts[1:])
    pieces = columns(q, q_far, v, v_far, kv_own, n_group, n_z, share, width)
    pieces = [pieces[0]] + exchange("member", 2, pieces[1:])
    own_avg = join_members(pieces, n_group, share, width)
    avg_near = gathered(own_avg, "group", 1)
    mid, *sends = token_mlp(
        row_parts,
        tok_near[:peers],
        w_out_tok,
        mlp_gain,
        ff_own + extra,
        ff_far + extra_far,
        ff_share,
    )
    received = exchange("group", 1, sends)
    lat_cols = latents if width % LANES == 0 else from_group(latents, width, 1)
    lat_new = latents_part(avg_near, lat_cols, ff_own, ff_far, ff_share)
    lat_parts = gathered(lat_new, "group", 1)
    return add_up(mid, received), place_columns(lat_parts)


def solution(mesh):
    in_specs = (
        P(("group", "member"), None),
        P("member", None),
        P(),
        P(),
        P(),
        P(),
        P(),
        P(),
        P("member", None),
        P("member", None),
        P("member", None),
        P(None, "member"),
        P("member", None),
    )
    out_specs = (P(("group", "member"), None), P("member", None))

    return jax.shard_map(per_device, mesh=mesh, in_specs=in_specs, out_specs=out_specs, check_vma=False)
```
